32 devices in a mesh: grp: 4 (over z), dev: 8 (over y, x, core).
Axes of the slice: x: 2, y: 2, z: 4, core: 2. Of those that a mesh axis runs over, the one named last changes fastest.
Arguments:
- integrals: bfloat16 [8, 1280, 1280], P('grp', 'dev'), may hold values from -0.15625 to 0.15625
- amplitudes: bfloat16 [8, 1280, 4, 192], P(None, 'grp', None, 'dev'), may hold values from -6 to 6
- occupied_energy: float32 [40], replicated, may hold values from -1.5 to -0.3
- virtual_energy: float32 [280], replicated, may hold values from 0.2 to 3
- virtual_pairs: int32 [8, 1280, 2], P('grp', 'dev'), may hold values from 0 to 279
- occupied_pairs: int32 [192, 2], replicated, may hold values from 0 to 39
Outputs:
- update: bfloat16 [8, 1280, 4, 192], P(None, 'dev', None, 'grp')
The draws below stay inside these ranges and needn't reach their ends.
All inputs are finite; a program needn't handle non-finite values.
Results may differ from the reference program's by a relative error of at most 0.001.
Values may be sent and summed in bfloat16 or wider, within the bound.
A program may use at most 64 MiB of HBM per device.

```python
import jax
import jax.numpy as jnp
from jax import lax

NVIR = 280
NOCC = 40
NBLK = 8
NAB = 1280
NIJ = 192
VEC = 4


def with_ends(entries, rng, low, high):
    extent = entries.shape
    spot = [jax.random.randint(jax.random.fold_in(rng, axis), (), 0, extent[axis]) for axis in range(len(extent))]
    entries = entries.at[tuple(spot)].set(low)
    longest = extent.index(max(extent))
    spot[longest] = (spot[longest] + 1) % extent[longest]
    return entries.at[tuple(spot)].set(high)


def steps_of(rng, dims, shards, least, largest):
    loudness = 1.0
    for axis_at, parts in shards:
        steps = jax.random.uniform(jax.random.fold_in(jax.random.fold_in(rng, 6), axis_at), (parts,), jnp.float32, least / len(shards), largest / len(shards))
        loudness = loudness * jnp.repeat(jnp.exp(steps), dims[axis_at] // parts).reshape((-1,) + (1,) * (len(dims) - 1 - axis_at))
    return loudness


def bell_draw(stream_key, shape, scale, bound, pieces=(), kind=jnp.bfloat16):
    entries = jax.random.normal(stream_key, shape, jnp.float32) * scale
    if len(pieces) > 0:
        entries = steps_of(stream_key, shape, pieces, -0.22, 0.18) * entries
    return jnp.clip(entries, min=-bound, max=bound).astype(kind)


def setup_inputs(seed: int = 0) -> dict:
    splits = jax.random.split(jax.random.key(seed), 7)
    return {
        "integrals": bell_draw(splits[0], (NBLK, NAB, NAB), NAB ** -0.5, 0.15625, ((0, 4), (1, 8))),
        "amplitudes": bell_draw(splits[1], (NBLK, NAB, VEC, NIJ), 1.0, 6.0, ((1, 4), (3, 8))),
        "occupied_energy": jnp.clip(jax.random.uniform(splits[2], (NOCC,), jnp.float32, -1.5, -0.3), -1.5, -0.3),
        "virtual_energy": jnp.clip(jax.random.uniform(splits[3], (NVIR,), jnp.float32, 0.2, 3.0), 0.2, 3.0),
        "virtual_pairs": with_ends(jax.random.randint(splits[4], (NBLK, NAB, 2), 0, NVIR), jax.random.fold_in(splits[4], 1), 0, NVIR - 1).astype(jnp.int32),
        "occupied_pairs": with_ends(jax.random.randint(splits[5], (NIJ, 2), 0, NOCC), jax.random.fold_in(splits[5], 1), 0, NOCC - 1).astype(jnp.int32),
    }


def reference(integrals, amplitudes, occupied_energy, virtual_energy, virtual_pairs, occupied_pairs):
    occ_sum = occupied_energy[occupied_pairs[:, 0]] + occupied_energy[occupied_pairs[:, 1]]

    def one_block(items):
        block_ints, block_amps, block_pairs = items
        rows = block_amps.shape[0]
        flat = block_amps.reshape(rows, -1).astype(jnp.float32)
        ladder = jnp.dot(block_ints.astype(jnp.float32), flat, preferred_element_type=jnp.float32)
        ladder = ladder.reshape(block_amps.shape)
        virt_sum = virtual_energy[block_pairs[:, 0]] + virtual_energy[block_pairs[:, 1]]
        denominator = occ_sum[None, :] - virt_sum[:, None]
        return (ladder / denominator[:, None, :]).astype(jnp.bfloat16)

    return lax.map(one_block, (integrals, amplitudes, virtual_pairs))
```

```python
import functools

import jax
import jax.numpy as jnp
from jax import lax
from jax.experimental import pallas as pl
from jax.experimental.pallas import tpu as pltpu
from jax.sharding import PartitionSpec as P

LANES = 128
F32 = jnp.float32
BF16 = jnp.bfloat16


def lookup(energy, indices):
    labels = jnp.arange(energy.shape[0], dtype=jnp.int32)
    picked = indices[:, None] == labels[None, :]
    return jnp.sum(jnp.where(picked, energy[None, :], 0.0), axis=1)


def plain(integrals, amplitudes, occupied_energy, virtual_energy, virtual_pairs, occupied_pairs):
    arrived = lax.all_to_all(amplitudes, "grp", split_axis=0, concat_axis=1, tiled=True)
    occ_sum = lookup(occupied_energy, occupied_pairs[:, 0]) + lookup(
        occupied_energy, occupied_pairs[:, 1]
    )
    results = []
    for block in range(arrived.shape[0]):
        panel = arrived[block]
        block_ints = integrals[block]
        gathered = lax.all_gather(panel, "dev", axis=2, tiled=True)
        ladder = jnp.einsum("ae,evj->avj", block_ints, gathered, preferred_element_type=jnp.float32)
        pairs_here = virtual_pairs[block]
        virt_sum = lookup(virtual_energy, pairs_here[:, 0]) + lookup(
            virtual_energy, pairs_here[:, 1]
        )
        denominator = occ_sum[None, :] - virt_sum[:, None]
        results.append((ladder / denominator[:, None, :]).astype(jnp.bfloat16))
    stacked = jnp.stack(results)
    return lax.all_to_all(stacked, "grp", split_axis=3, concat_axis=0, tiled=True)


def as_column(row):
    n = row.shape[1]
    eye = lax.broadcasted_iota(jnp.int32, (n, n), 0) == lax.broadcasted_iota(jnp.int32, (n, n), 1)
    return jnp.sum(jnp.where(eye, jnp.broadcast_to(row, (n, n)), 0.0), axis=1, keepdims=True)


def picked_row(column, index_row):
    shape = (column.shape[0], index_row.shape[1])
    hit = lax.broadcasted_iota(jnp.int32, shape, 0) == jnp.broadcast_to(index_row, shape)
    return jnp.sum(jnp.where(hit, jnp.broadcast_to(column, shape), 0.0), axis=0, keepdims=True)


def body(
    dims,
    ints_hbm,
    amps_hbm,
    occ_e_hbm,
    virt_e_hbm,
    vpairs_hbm,
    opairs_hbm,
    out,
    ints,
    amps,
    occ_e,
    virt_e,
    vpairs,
    opairs,
    packed,
    gath,
    other_ints,
    other_pairs,
    weights,
    recip,
    occ_col,
    sendbuf,
    recvbuf,
    z_send,
    z_recv,
    xy_send,
    xy_recv,
    o_send,
    o_recv,
    pair_send,
    pair_recv,
    load_amps,
    load_rest,
):
    groups, blocks_here, vec, nij, nab, nef = dims
    rows = vec * nij
    half = rows // 2
    tail = nef % LANES
    chunk = packed.shape[1]
    cut = chunk // 32 * 16
    z = lax.axis_index("grp")
    dev = lax.axis_index("dev")
    core = dev % 2
    chip = dev // 2
    flip_x = chip + 1 - 2 * (chip % 2)
    flip_y = chip + 2 - 4 * (chip // 2)
    mesh_id = pl.DeviceIdType.MESH

    def at(zz, pp, cc):
        return (zz, pp * 2 + cc)

    low = z < groups // 2

    def far(step):
        down = groups - 1 - step
        down = down - jnp.where(down <= z, 1, 0)
        up = step + jnp.where(step >= z, 1, 0)
        return jnp.where(low, down, up)

    barrier = pltpu.get_barrier_semaphore()
    peers = [at(z, chip, 1 - core), at(z, flip_x, core), at(z, flip_y, core)]
    for s in range(groups - 1):
        peers.append(at(far(s), chip, core))
        peers.append(at(far(s), chip, 1 - core))
    for peer in peers:
        pl.semaphore_signal(barrier, inc=1, device_id=peer, device_id_type=mesh_id)

    loads = []
    for blk in range(packed.shape[0]):
        loads.append(pltpu.make_async_copy(amps_hbm.at[blk], amps.at[blk], load_amps.at[blk]))
    pairs = [(ints_hbm, ints), (occ_e_hbm, occ_e), (virt_e_hbm, virt_e), (vpairs_hbm, vpairs), (opairs_hbm, opairs)]
    rest = [pltpu.make_async_copy(src, dst, load_rest.at[i]) for i, (src, dst) in enumerate(pairs)]
    for load in loads + rest:
        load.start()

    for blk in range(packed.shape[0]):
        loads[blk].wait()
        packed[blk, 0:rows, :] = amps[blk, :, 0:LANES]
        packed[blk, rows : 2 * rows, :] = amps[blk, :, LANES : 2 * LANES]
        left = amps[blk, 0:half, 2 * LANES : nef].astype(F32)
        right = amps[blk, half:rows, 2 * LANES : nef].astype(F32)
        packed[blk, 2 * rows : chunk, :] = jnp.concatenate([left, right], axis=1).astype(BF16)

    pl.semaphore_wait(barrier, len(peers))

    started = []

    def send(src, dst, ssem, rsem, to):
        copy = pltpu.make_async_remote_copy(
            src_ref=src, dst_ref=dst, send_sem=ssem, recv_sem=rsem, device_id=to, device_id_type=mesh_id
        )
        copy.start()
        started.append(copy)
        return copy

    for b in range(blocks_here):
        for s in range(groups - 1):
            to = far(s)
            send(
                packed.at[to * blocks_here + b],
                gath.at[b, z, chip],
                z_send.at[b, s],
                z_recv.at[b, z],
                at(to, chip, core),
            )

    def arrived(ref, sem):
        pltpu.make_async_remote_copy(
            src_ref=ref, dst_ref=ref, send_sem=sem, recv_sem=sem,
            device_id=at(z, chip, 1 - core), device_id_type=mesh_id,
        ).wait_recv()

    order = [(b, None) for b in range(blocks_here)]
    order += [(b, s) for b in range(blocks_here) for s in range(groups - 1)]

    def source(s):
        return z if s is None else far(s)

    def first(k):
        b, s = order[k]
        zz = source(s)
        src = gath.at[b, zz, chip]
        if s is None:
            src = packed.at[z * blocks_here + b]
        else:
            arrived(src, z_recv.at[b, zz])
        send(src, gath.at[b, zz, chip], xy_send.at[k, 0], xy_recv.at[b, zz, 0], at(z, flip_x, core))
        send(src, gath.at[b, zz, chip], xy_send.at[k, 1], xy_recv.at[b, zz, 1], at(z, flip_y, core))

    def second(k):
        b, s = order[k]
        zz = source(s)
        arrived(gath.at[b, zz, flip_x], xy_recv.at[b, zz, 0])
        src = gath.at[b, zz, flip_x, 0:cut]
        send(src, src, xy_send.at[k, 2], xy_recv.at[b, zz, 2], at(z, flip_y, core))
        arrived(gath.at[b, zz, flip_y], xy_recv.at[b, zz, 1])
        src = gath.at[b, zz, flip_y, cut:chunk]
        send(src, src, xy_send.at[k, 3], xy_recv.at[b, zz, 3], at(z, flip_x, core))

    def third(k):
        b, s = order[k]
        zz = source(s)
        diag = 3 - chip
        arrived(gath.at[b, zz, diag, 0:cut], xy_recv.at[b, zz, 2])
        arrived(gath.at[b, zz, diag, cut:chunk], xy_recv.at[b, zz, 3])

    for k in range(blocks_here):
        first(k)
    partner = at(z, chip, 1 - core)
    for load in rest:
        load.wait()
    send(vpairs, other_pairs, pair_send.at[0], pair_recv.at[0], partner)
    send(ints, other_ints, pair_send.at[1], pair_recv.at[1], partner)

    for b in range(blocks_here):
        gath[b, z, chip] = packed[z * blocks_here + b]

    occ_column = as_column(occ_e[...].reshape(1, -1))
    occ_row = picked_row(occ_column, opairs[0:1, :]) + picked_row(occ_column, opairs[1:2, :])
    occ_col[...] = jnp.broadcast_to(as_column(occ_row), occ_col.shape)
    virt_column = as_column(virt_e[...].reshape(1, -1))

    def prepare(side, int_ref, pair_ref):
        for b in range(blocks_here):
            virt_row = picked_row(virt_column, pair_ref[b, 0:1, :]) + picked_row(
                virt_column, pair_ref[b, 1:2, :]
            )
            for p in range(gath.shape[2]):
                start = pl.multiple_of((2 * p + core) * nij, 8)
                occ = occ_col[pl.ds(start, nij), 0:1]
                recip[b, side, p] = 1.0 / (occ - virt_row)
            for zz in range(groups):
                panel = int_ref[b, :, zz * nef : (zz + 1) * nef].astype(F32)
                last = panel[:, 2 * LANES : nef]
                wide = jnp.concatenate([panel[:, 0 : 2 * LANES], last, last], axis=1)
                width = 3 * LANES
                weights[b, side, :, zz * width : (zz + 1) * width] = wide.astype(BF16)

    second(0)
    prepare(0, ints, vpairs)
    later = blocks_here
    first(later)
    second(1)
    first(later + 1)
    arrived(other_pairs, pair_recv.at[0])
    arrived(other_ints, pair_recv.at[1])
    prepare(1, other_ints, other_pairs)

    chips = gath.shape[2]
    lane = lax.broadcasted_iota(jnp.int32, (half, LANES), 1)
    main_lanes = nab // LANES * LANES

    def compute(b):
        parts = []
        for zz in range(groups):
            per_chip = []
            for p in range(chips):
                end = gath[b, zz, p, 2 * rows : chunk, :]
                zero = jnp.zeros_like(end)
                end2 = jnp.concatenate(
                    [jnp.where(lane < tail, end, zero), jnp.where(lane < tail, zero, end)], axis=0
                )
                per_chip.append(
                    jnp.concatenate([gath[b, zz, p, 0:rows, :], gath[b, zz, p, rows : 2 * rows, :], end2], axis=1)
                )
            parts.append(jnp.concatenate(per_chip, axis=0))
        left = jnp.concatenate(parts, axis=1)
        for side in range(2):
            total = lax.dot_general(
                left, weights[b, side], (((1,), (1,)), ((), ())), preferred_element_type=F32
            )
            scaled = total.reshape(chips, vec, nij, nab) * recip[b, side][:, None]
            to_core = jnp.where(side == 0, core, 1 - core)
            for p in range(chips):
                ends = [scaled[p, v, :, main_lanes:nab] for v in range(vec)]
                sendbuf[b, p, side, 0:rows, :] = scaled[p, :, :, 0:main_lanes].reshape(rows, main_lanes).astype(BF16)
                sendbuf[b, p, side, rows : rows + nij, :] = jnp.concatenate(ends, axis=1).astype(BF16)
        for s in range(groups - 1):
            to = far(s)
            for side in range(2):
                send(
                    sendbuf.at[b, to, side], recvbuf.at[z, b, core],
                    o_send.at[b, s, side], o_recv.at[z, b, core],
                    at(to, chip, core if side == 0 else 1 - core),
                )
        send(
            sendbuf.at[b, z, 1], recvbuf.at[z, b, core],
            o_send.at[b, groups - 1, 1], o_recv.at[z, b, core], partner,
        )
        recvbuf[z, b, core] = sendbuf[b, z, 0]

    def unpack(zz, b):
        got = [recvbuf[zz, b, c].astype(F32) for c in range(2)]
        width = nab - main_lanes
        for v in range(vec):
            pieces = []
            for c in range(2):
                main = got[c][v * nij : (v + 1) * nij, :]
                end = got[c][rows : rows + nij, v * width : (v + 1) * width]
                pieces.append(jnp.concatenate([main, end], axis=1))
            out[zz * blocks_here + b, v] = jnp.concatenate(pieces, axis=0).astype(BF16)

    steps = len(order)
    per = groups - 1
    first(later + 2)
    pos = later + 3
    done = 2
    ready = {b: later + (b + 1) * per for b in range(blocks_here)}
    for b in range(blocks_here):
        while done < ready[b]:
            if pos < steps:
                first(pos)
                pos += 1
            second(done)
            done += 1
        third(b)
        for k in range(later + b * per, later + (b + 1) * per):
            third(k)
        compute(b)

    for b in range(blocks_here):
        arrived(recvbuf.at[z, b, 1 - core], o_recv.at[z, b, 1 - core])
        unpack(z, b)
        for s in range(groups - 1):
            zz = far(s)
            for c in range(2):
                arrived(recvbuf.at[zz, b, c], o_recv.at[zz, b, c])
            unpack(zz, b)
    for copy in started:
        copy.wait_send()


def fused(groups, integrals, amplitudes, occupied_energy, virtual_energy, virtual_pairs, occupied_pairs):
    nblk, nef, vec, nij = amplitudes.shape
    here, nab, _ = integrals.shape
    rows = vec * nij
    chips = lax.axis_size("dev") // 2
    amps = jnp.transpose(amplitudes, (0, 2, 3, 1)).reshape(nblk, rows, nef)
    vpairs = jnp.transpose(virtual_pairs, (0, 2, 1))
    opairs = jnp.transpose(occupied_pairs, (1, 0))
    chunk = 2 * rows + rows // 2
    dims = (groups, here, vec, nij, nab, nef)
    dma = pltpu.SemaphoreType.DMA
    nchunks = here * groups
    arrays = (integrals, amps, occupied_energy, virtual_energy, vpairs, opairs)
    result = pl.pallas_call(
        functools.partial(body, dims),
        out_shape=jax.ShapeDtypeStruct((nblk, vec, 2 * nij, nab), BF16),
        in_specs=[pl.BlockSpec(memory_space=pltpu.HBM)] * 6,
        out_specs=pl.BlockSpec(memory_space=pltpu.VMEM),
        scratch_shapes=[
            pltpu.VMEM(integrals.shape, BF16),
            pltpu.VMEM(amps.shape, BF16),
            pltpu.VMEM(occupied_energy.shape, F32),
            pltpu.VMEM(virtual_energy.shape, F32),
            pltpu.VMEM(vpairs.shape, jnp.int32),
            pltpu.VMEM(opairs.shape, jnp.int32),
            pltpu.VMEM((nblk, chunk, LANES), BF16),
            pltpu.VMEM((here, groups, chips, chunk, LANES), BF16),
            pltpu.VMEM(integrals.shape, BF16),
            pltpu.VMEM(vpairs.shape, jnp.int32),
            pltpu.VMEM((here, 2, nab, groups * 3 * LANES), BF16),
            pltpu.VMEM((here, 2, chips, nij, nab), F32),
            pltpu.VMEM((2 * chips * nij, LANES), F32),
            pltpu.VMEM((here, groups, 2, rows + nij, LANES), BF16),
            pltpu.VMEM((groups, here, 2, rows + nij, LANES), BF16),
            dma((here, groups - 1)),
            dma((here, groups)),
            dma((nchunks, 4)),
            dma((here, groups, 4)),
            dma((here, groups, 2)),
            dma((groups, here, 2)),
            dma((2,)),
            dma((2,)),
            dma((nblk,)),
            dma((5,)),
        ],
        compiler_params=pltpu.CompilerParams(
            collective_id=0, has_side_effects=True, vmem_limit_bytes=32 * 1024 * 1024
        ),
        name="ladder",
    )(*[pltpu.with_memory_space_constraint(array, pltpu.HBM) for array in arrays])
    return jnp.transpose(result, (0, 3, 1, 2))


def solution(mesh):
    placed = (
        P("grp", "dev", None),
        P(None, "grp", None, "dev"),
        P(),
        P(),
        P("grp", "dev", None),
        P(),
    )
    groups, devs = mesh.shape["grp"], mesh.shape["dev"]

    def local(integrals, amplitudes, *rest):
        nef, vec, nij = amplitudes.shape[1:]
        nab = integrals.shape[1]
        square = devs == 2 * 2 * 2 and devs == 2 * groups
        packs = (
            2 * LANES < nef < 3 * LANES
            and 2 * (nef % LANES) == LANES
            and LANES < nab < 2 * LANES
            and vec * (nab % LANES) == LANES
            and nij % 8 == 0
            and (vec * nij) % 32 == 0
        )
        if square and packs:
            return fused(groups, integrals, amplitudes, *rest)
        return plain(integrals, amplitudes, *rest)

    return jax.shard_map(
        local, mesh=mesh, in_specs=placed, out_specs=P(None, "dev", None, "grp"), check_vma=False
    )
```

```python
import functools

import jax
import jax.numpy as jnp
from jax import lax
from jax.experimental import pallas as pl
from jax.experimental.pallas import tpu as pltpu
from jax.sharding import PartitionSpec as P

LANES = 128
F32 = jnp.float32
BF16 = jnp.bfloat16


def lookup(energy, indices):
    labels = jnp.arange(energy.shape[0], dtype=jnp.int32)
    picked = indices[:, None] == labels[None, :]
    return jnp.sum(jnp.where(picked, energy[None, :], 0.0), axis=1)


def plain(integrals, amplitudes, occupied_energy, virtual_energy, virtual_pairs, occupied_pairs):
    arrived = lax.all_to_all(amplitudes, "grp", split_axis=0, concat_axis=1, tiled=True)
    occ_sum = lookup(occupied_energy, occupied_pairs[:, 0]) + lookup(
        occupied_energy, occupied_pairs[:, 1]
    )
    results = []
    for block in range(arrived.shape[0]):
        panel = arrived[block]
        block_ints = integrals[block]
        gathered = lax.all_gather(panel, "dev", axis=2, tiled=True)
        ladder = jnp.einsum("ae,evj->avj", block_ints, gathered, preferred_element_type=jnp.float32)
        pairs_here = virtual_pairs[block]
        virt_sum = lookup(virtual_energy, pairs_here[:, 0]) + lookup(
            virtual_energy, pairs_here[:, 1]
        )
        denominator = occ_sum[None, :] - virt_sum[:, None]
        results.append((ladder / denominator[:, None, :]).astype(jnp.bfloat16))
    stacked = jnp.stack(results)
    return lax.all_to_all(stacked, "grp", split_axis=3, concat_axis=0, tiled=True)


def as_column(row):
    n = row.shape[1]
    eye = lax.broadcasted_iota(jnp.int32, (n, n), 0) == lax.broadcasted_iota(jnp.int32, (n, n), 1)
    return jnp.sum(jnp.where(eye, jnp.broadcast_to(row, (n, n)), 0.0), axis=1, keepdims=True)


def picked_row(column, index_row):
    shape = (column.shape[0], index_row.shape[1])
    hit = lax.broadcasted_iota(jnp.int32, shape, 0) == jnp.broadcast_to(index_row, shape)
    return jnp.sum(jnp.where(hit, jnp.broadcast_to(column, shape), 0.0), axis=0, keepdims=True)


def body(
    dims,
    ints_hbm,
    amps_hbm,
    occ_e_hbm,
    virt_e_hbm,
    vpairs_hbm,
    opairs_hbm,
    out,
    ints,
    amps,
    occ_e,
    virt_e,
    vpairs,
    opairs,
    tails,
    gath,
    other_ints,
    other_pairs,
    weights,
    recip,
    occ_col,
    sendbuf,
    recvbuf,
    ready,
    z_send,
    z_recv,
    d_send,
    d_recv,
    f_send,
    f_recv,
    o_send,
    o_recv,
    pair_send,
    pair_recv,
    load_amps,
    load_own,
    load_rest,
):
    groups, blocks_here, vec, nij, nab, nef = dims
    rows = vec * nij
    half = rows // 2
    tail = nef % LANES
    main = nef - tail
    bulk = main // LANES * rows
    chunk = bulk + half
    cut = chunk // 32 * 16
    z = lax.axis_index("grp")
    dev = lax.axis_index("dev")
    core = dev % 2
    chip = dev // 2
    flip_x = chip + 1 - 2 * (chip % 2)
    flip_y = chip + 2 - 4 * (chip // 2)
    diag = 3 - chip
    mesh_id = pl.DeviceIdType.MESH

    def at(zz, pp, cc):
        return (zz, pp * 2 + cc)

    low = z < groups // 2

    def far(step):
        down = groups - 1 - step
        down = down - jnp.where(down <= z, 1, 0)
        up = step + jnp.where(step >= z, 1, 0)
        return jnp.where(low, down, up)

    def across(step):
        return jnp.where(low, groups // 2 + step, groups // 2 - 1 - step)

    def reach(step):
        return jnp.where(step < z, z - 1 - step, step + 1)

    loads = []
    for b in range(blocks_here):
        loads.append(pltpu.make_async_copy(amps_hbm.at[z * blocks_here + b], amps.at[b], load_amps.at[0]))
    for s in range(groups - 1):
        for b in range(blocks_here):
            slot = (s + 1) * blocks_here + b
            loads.append(
                pltpu.make_async_copy(amps_hbm.at[reach(s) * blocks_here + b], amps.at[slot], load_amps.at[1])
            )

    def bulk_parts(block, piece):
        for i in range(main // LANES):
            yield amps_hbm.at[block, :, i * LANES : (i + 1) * LANES], piece.at[i * rows : (i + 1) * rows]

    for b in range(blocks_here):
        for src, dst in bulk_parts(z * blocks_here + b, gath.at[b, z, chip]):
            loads.append(pltpu.make_async_copy(src, dst, load_own.at[0]))
    pairs = [(ints_hbm, ints), (occ_e_hbm, occ_e), (virt_e_hbm, virt_e), (vpairs_hbm, vpairs), (opairs_hbm, opairs)]
    rest = [pltpu.make_async_copy(src, dst, load_rest.at[i]) for i, (src, dst) in enumerate(pairs)]

    partner = at(z, chip, 1 - core)
    x_peer = at(z, flip_x, core)
    y_peer = at(z, flip_y, core)
    swap = chip == 2
    ways = [
        at(z, jnp.where(swap, flip_y, flip_x), core),
        at(z, jnp.where(swap, flip_x, flip_y), core),
    ]
    peers = [(partner, core == 0, 0), (x_peer, chip % 2 == 0, 1), (y_peer, chip < 2, 2)]
    for s in range(groups - 1):
        zz = reach(s)
        for c in range(2):
            peers.append((at(zz, chip, core if c == 0 else 1 - core), zz > z, 3 + s * 2 + c))
    barrier = pltpu.get_barrier_semaphore()
    for peer, higher, _ in peers:
        @pl.when(higher)
        def _(peer=peer):
            pl.semaphore_signal(barrier, inc=1, device_id=peer, device_id_type=mesh_id)
    for load in loads + rest:
        load.start()
    earlier = 2 * z + chip % 2 + chip // 2 + core

    @pl.when(earlier > 0)
    def _():
        pl.semaphore_wait(barrier, earlier)

    for i, (peer, higher, slot) in enumerate(peers):
        if i < 3:
            there = slot
        else:
            s, c = (i - 3) // 2, (i - 3) % 2
            zz = reach(s)
            there = 3 + c + 2 * jnp.where(z < zz, zz - 1 - z, z - 1)

        @pl.when(jnp.logical_not(higher))
        def _(peer=peer, there=there):
            pl.semaphore_signal(ready.at[there], inc=1, device_id=peer, device_id_type=mesh_id)

    def met(i):
        @pl.when(peers[i][1])
        def _():
            pl.semaphore_wait(ready.at[peers[i][2]], 1)

    def met_way(way):
        i = jnp.where(swap, 2 - way, 1 + way)
        higher = jnp.where(i == 1, chip % 2 == 0, chip < 2)

        @pl.when(higher)
        def _():
            pl.semaphore_wait(ready.at[i], 1)

    def send(src, dst, ssem, rsem, to):
        pltpu.make_async_remote_copy(
            src_ref=src, dst_ref=dst, send_sem=ssem, recv_sem=rsem, device_id=to, device_id_type=mesh_id
        ).start()

    def whole(ref, sem):
        return pltpu.make_async_remote_copy(
            src_ref=ref, dst_ref=ref, send_sem=sem, recv_sem=sem, device_id=partner, device_id_type=mesh_id
        )

    def arrived(ref, sem):
        whole(ref, sem).wait_recv()

    def left(ref, sem):
        whole(ref, sem).wait_send()

    order = [(b, s) for s in (0, 1) for b in range(blocks_here)]
    order += [(b, s) for b in range(blocks_here) for s in range(2, groups)]

    def source(s):
        if s < 2:
            return z if s == 0 else z + 1 - 2 * (z % 2)
        return across(s - 2)

    def direct_main(b, way):
        for src, dst in bulk_parts(z * blocks_here + b, gath.at[b, z, chip]):
            send(src, dst, d_send.at[0], d_recv.at[b, z], ways[way])

    def direct_tail(b, way):
        send(tails.at[b], gath.at[b, z, chip, bulk:chunk], d_send.at[0], d_recv.at[b, z], ways[way])

    def inward_main(b, s):
        to = reach(s)
        for src, dst in bulk_parts(to * blocks_here + b, gath.at[b, z, chip]):
            send(src, dst, z_send.at[0], z_recv.at[b, z], at(to, chip, core))

    def inward_tail(b, s):
        to = reach(s)
        send(
            tails.at[(s + 1) * blocks_here + b], gath.at[b, z, chip, bulk:chunk],
            z_send.at[0], z_recv.at[b, z], at(to, chip, core),
        )

    def first(k):
        b, s = order[k]
        zz = source(s)
        piece = gath.at[b, zz, chip]
        arrived(piece, z_recv.at[b, zz])
        for peer in (x_peer, y_peer):
            send(piece, piece, d_send.at[0], d_recv.at[b, zz], peer)

    def second(k):
        b, s = order[k]
        zz = source(s)
        arrived(gath.at[b, zz, 0:2], d_recv.at[b, zz])
        src = gath.at[b, zz, flip_x, 0:cut]
        send(src, src, f_send.at[0], f_recv.at[b], y_peer)
        src = gath.at[b, zz, flip_y, cut:chunk]
        send(src, src, f_send.at[0], f_recv.at[b], x_peer)

    def third(b):
        arrived(gath.at[b, :, diag], f_recv.at[b])

    def pack(slot):
        lower = amps[slot, 0:half, main:nef].astype(F32)
        upper = amps[slot, half:rows, main:nef].astype(F32)
        tails[slot] = jnp.concatenate([lower, upper], axis=1).astype(BF16)

    def loaded(slots, sem):
        pltpu.make_async_copy(amps.at[slots], amps.at[slots], sem).wait()

    met_way(0)
    direct_main(0, 0)
    met_way(1)
    direct_main(0, 1)
    met(3)
    inward_main(0, 0)
    loaded(slice(0, blocks_here), load_amps.at[0])
    for b in range(blocks_here):
        pack(b)
    for b in range(blocks_here):
        if b > 0:
            direct_main(b, 0)
            direct_main(b, 1)
        direct_tail(b, 0)
        direct_tail(b, 1)
    loaded(slice(blocks_here, groups * blocks_here), load_amps.at[1])
    for slot in range(blocks_here, groups * blocks_here):
        pack(slot)
    inward_tail(0, 0)
    for s in range(1, groups - 1):
        met(3 + 2 * s)
        inward_main(0, s)
        inward_tail(0, s)
    for b in range(1, blocks_here):
        for s in range(groups - 1):
            inward_main(b, s)
            inward_tail(b, s)
    met(0)
    send(vpairs_hbm, other_pairs, pair_send.at[0], pair_recv.at[0], partner)
    send(ints_hbm, other_ints, pair_send.at[1], pair_recv.at[1], partner)
    for b in range(blocks_here):
        gath[b, z, chip, bulk:chunk] = tails[b]
    for load in rest:
        load.wait()

    occ_column = as_column(occ_e[...].reshape(1, -1))
    occ_row = picked_row(occ_column, opairs[0:1, :]) + picked_row(occ_column, opairs[1:2, :])
    occ_col[...] = jnp.broadcast_to(as_column(occ_row), occ_col.shape)
    virt_column = as_column(virt_e[...].reshape(1, -1))

    def prepare(side, int_ref, pair_ref):
        for b in range(blocks_here):
            virt_row = picked_row(virt_column, pair_ref[b, 0:1, :]) + picked_row(
                virt_column, pair_ref[b, 1:2, :]
            )
            for p in range(gath.shape[2]):
                start = pl.multiple_of((2 * p + core) * nij, 8)
                occ = occ_col[pl.ds(start, nij), 0:1]
                recip[b, side, p] = 1.0 / (occ - virt_row)
            for zz in range(groups):
                panel = int_ref[b, :, zz * nef : (zz + 1) * nef].astype(F32)
                last = panel[:, main:nef]
                wide = jnp.concatenate([panel[:, 0:main], last, last], axis=1)
                width = main + LANES
                weights[b, side, :, zz * width : (zz + 1) * width] = wide.astype(BF16)

    lane = lax.broadcasted_iota(jnp.int32, (half, LANES), 1)
    main_lanes = nab // LANES * LANES

    def job(b, p):
        parts = []
        for zz in range(groups):
            end = gath[b, zz, p, bulk:chunk]
            zero = jnp.zeros_like(end)
            end2 = jnp.concatenate(
                [jnp.where(lane < tail, end, zero), jnp.where(lane < tail, zero, end)], axis=0
            )
            parts += [gath[b, zz, p, i * rows : (i + 1) * rows] for i in range(main // LANES)] + [end2]
        panel = jnp.concatenate(parts, axis=1)
        for side in range(2):
            total = lax.dot_general(
                panel, weights[b, side], (((1,), (1,)), ((), ())), preferred_element_type=F32
            )
            scaled = total.reshape(vec, nij, nab) * recip[b, side, p][None]
            ends = [scaled[v, :, main_lanes:nab] for v in range(vec)]
            sendbuf[b, p, side, 0:rows, :] = scaled[:, :, 0:main_lanes].reshape(rows, main_lanes).astype(BF16)
            sendbuf[b, p, side, rows : rows + nij, :] = jnp.concatenate(ends, axis=1).astype(BF16)

        @pl.when(p != z)
        def _():
            for side in range(2):
                send(
                    sendbuf.at[b, p, side], recvbuf.at[z, b, core], o_send.at[0], o_recv.at[z, b],
                    at(p, chip, core if side == 0 else 1 - core),
                )

        @pl.when(p == z)
        def _():
            send(sendbuf.at[b, z, 1], recvbuf.at[z, b, core], o_send.at[1], o_recv.at[z, b], partner)
            recvbuf[z, b, core] = sendbuf[b, z, 0]

    wanted = [far(s) for s in range(groups - 1)] + [z]
    spot = sum(jnp.where(wanted[i] == diag, i, 0) for i in range(groups))
    late = [jnp.where(i >= spot, wanted[i + 1], wanted[i]) for i in range(groups - 1)] + [diag]

    def unpack(zz, b):
        got = [recvbuf[zz, b, c].astype(F32) for c in range(2)]
        width = nab - main_lanes
        for v in range(vec):
            pieces = []
            for c in range(2):
                body_rows = got[c][v * nij : (v + 1) * nij, :]
                end = got[c][rows : rows + nij, v * width : (v + 1) * width]
                pieces.append(jnp.concatenate([body_rows, end], axis=1))
            out[zz * blocks_here + b, v] = jnp.concatenate(pieces, axis=0).astype(BF16)

    prepare(0, ints, vpairs)
    second(0)
    first(2)
    second(1)
    arrived(other_pairs, pair_recv.at[0])
    arrived(other_ints, pair_recv.at[1])
    prepare(1, other_ints, other_pairs)
    first(3)
    first(4)
    second(2)
    first(5)
    second(4)
    second(5)
    pltpu.make_async_copy(gath.at[:, z, chip, 0:bulk], gath.at[:, z, chip, 0:bulk], load_own.at[0]).wait()
    for s in range(groups - 1):
        met(4 + 2 * s)
    job(0, late[0])
    job(0, late[1])
    first(6)
    job(0, late[2])
    first(7)
    second(3)
    third(0)
    job(0, late[3])
    second(6)
    second(7)
    for i in range(groups - 1):
        job(1, late[i])
    third(1)
    job(1, late[groups - 1])

    for b in range(blocks_here):
        arrived(recvbuf.at[z, b, 1 - core], o_recv.at[z, b])
        unpack(z, b)
        for s in range(groups - 1):
            zz = far(s)
            arrived(recvbuf.at[zz, b], o_recv.at[zz, b])
            unpack(zz, b)
    left(gath.at[:, 0 : groups - 1, 0], z_send.at[0])
    left(gath.at[0], d_send.at[0])
    left(gath.at[:, :, 0], f_send.at[0])
    left(sendbuf.at[:, 0 : groups - 1], o_send.at[0])
    left(sendbuf.at[:, 0, 0], o_send.at[1])
    left(other_pairs, pair_send.at[0])
    left(other_ints, pair_send.at[1])


def fused(groups, integrals, amplitudes, occupied_energy, virtual_energy, virtual_pairs, occupied_pairs):
    nblk, nef, vec, nij = amplitudes.shape
    here, nab, _ = integrals.shape
    rows = vec * nij
    chips = lax.axis_size("dev") // 2
    amps = jnp.transpose(amplitudes, (0, 2, 3, 1)).reshape(nblk, rows, nef)
    vpairs = jnp.transpose(virtual_pairs, (0, 2, 1))
    opairs = jnp.transpose(occupied_pairs, (1, 0))
    dims = (groups, here, vec, nij, nab, nef)
    dma = pltpu.SemaphoreType.DMA
    arrays = (integrals, amps, occupied_energy, virtual_energy, vpairs, opairs)
    result = pl.pallas_call(
        functools.partial(body, dims),
        out_shape=jax.ShapeDtypeStruct((nblk, vec, 2 * nij, nab), BF16),
        in_specs=[pl.BlockSpec(memory_space=pltpu.HBM)] * 6,
        out_specs=pl.BlockSpec(memory_space=pltpu.VMEM),
        scratch_shapes=[
            pltpu.VMEM(integrals.shape, BF16),
            pltpu.VMEM(amps.shape, BF16),
            pltpu.VMEM(occupied_energy.shape, F32),
            pltpu.VMEM(virtual_energy.shape, F32),
            pltpu.VMEM(vpairs.shape, jnp.int32),
            pltpu.VMEM(opairs.shape, jnp.int32),
            pltpu.VMEM((nblk, rows // 2, LANES), BF16),
            pltpu.VMEM((here, groups, chips, 2 * rows + rows // 2, LANES), BF16),
            pltpu.VMEM(integrals.shape, BF16),
            pltpu.VMEM(vpairs.shape, jnp.int32),
            pltpu.VMEM((here, 2, nab, groups * 3 * LANES), BF16),
            pltpu.VMEM((here, 2, chips, nij, nab), F32),
            pltpu.VMEM((2 * chips * nij, LANES), F32),
            pltpu.VMEM((here, groups, 2, rows + nij, LANES), BF16),
            pltpu.VMEM((groups, here, 2, rows + nij, LANES), BF16),
            pltpu.SemaphoreType.REGULAR((3 + 2 * (groups - 1),)),
            dma((1,)),
            dma((here, groups)),
            dma((1,)),
            dma((here, groups)),
            dma((1,)),
            dma((here,)),
            dma((2,)),
            dma((groups, here)),
            dma((2,)),
            dma((2,)),
            dma((2,)),
            dma((1,)),
            dma((5,)),
        ],
        compiler_params=pltpu.CompilerParams(
            collective_id=0, has_side_effects=True, vmem_limit_bytes=32 * 1024 * 1024
        ),
        name="ladder",
    )(*[pltpu.with_memory_space_constraint(array, pltpu.HBM) for array in arrays])
    return jnp.transpose(result, (0, 3, 1, 2))


def solution(mesh):
    placed = (
        P("grp", "dev", None),
        P(None, "grp", None, "dev"),
        P(),
        P(),
        P("grp", "dev", None),
        P(),
    )
    groups, devs = mesh.shape["grp"], mesh.shape["dev"]

    def local(integrals, amplitudes, *rest):
        nef, vec, nij = amplitudes.shape[1:]
        nab = integrals.shape[1]
        square = devs == 2 * 2 * 2 and devs == 2 * groups
        packs = (
            2 * LANES < nef < 3 * LANES
            and 2 * (nef % LANES) == LANES
            and LANES < nab < 2 * LANES
            and vec * (nab % LANES) == LANES
            and nij % 8 == 0
            and (vec * nij) % 32 == 0
        )
        if square and packs:
            return fused(groups, integrals, amplitudes, *rest)
        return plain(integrals, amplitudes, *rest)

    return jax.shard_map(
        local, mesh=mesh, in_specs=placed, out_specs=P(None, "dev", None, "grp"), check_vma=False
    )
```

```python
import functools

import jax
import jax.numpy as jnp
from jax import lax
from jax.experimental import pallas as pl
from jax.experimental.pallas import tpu as pltpu
from jax.sharding import PartitionSpec as P

LANES = 128
F32 = jnp.float32
BF16 = jnp.bfloat16


def lookup(energy, indices):
    labels = jnp.arange(energy.shape[0], dtype=jnp.int32)
    picked = indices[:, None] == labels[None, :]
    return jnp.sum(jnp.where(picked, energy[None, :], 0.0), axis=1)


def plain(integrals, amplitudes, occupied_energy, virtual_energy, virtual_pairs, occupied_pairs):
    arrived = lax.all_to_all(amplitudes, "grp", split_axis=0, concat_axis=1, tiled=True)
    occ_sum = lookup(occupied_energy, occupied_pairs[:, 0]) + lookup(
        occupied_energy, occupied_pairs[:, 1]
    )
    results = []
    for block in range(arrived.shape[0]):
        panel = arrived[block]
        block_ints = integrals[block]
        gathered = lax.all_gather(panel, "dev", axis=2, tiled=True)
        ladder = jnp.einsum("ae,evj->avj", block_ints, gathered, preferred_element_type=jnp.float32)
        pairs_here = virtual_pairs[block]
        virt_sum = lookup(virtual_energy, pairs_here[:, 0]) + lookup(
            virtual_energy, pairs_here[:, 1]
        )
        denominator = occ_sum[None, :] - virt_sum[:, None]
        results.append((ladder / denominator[:, None, :]).astype(jnp.bfloat16))
    stacked = jnp.stack(results)
    return lax.all_to_all(stacked, "grp", split_axis=3, concat_axis=0, tiled=True)


def as_column(row):
    n = row.shape[1]
    eye = lax.broadcasted_iota(jnp.int32, (n, n), 0) == lax.broadcasted_iota(jnp.int32, (n, n), 1)
    return jnp.sum(jnp.where(eye, jnp.broadcast_to(row, (n, n)), 0.0), axis=1, keepdims=True)


def picked_row(column, index_row):
    shape = (column.shape[0], index_row.shape[1])
    hit = lax.broadcasted_iota(jnp.int32, shape, 0) == jnp.broadcast_to(index_row, shape)
    return jnp.sum(jnp.where(hit, jnp.broadcast_to(column, shape), 0.0), axis=0, keepdims=True)


def body(
    dims,
    ints_hbm,
    amps_hbm,
    occ_e_hbm,
    virt_e_hbm,
    vpairs_hbm,
    opairs_hbm,
    out,
    ints,
    amps,
    occ_e,
    virt_e,
    vpairs,
    opairs,
    tails,
    gath,
    other_ints,
    other_pairs,
    weights,
    recip,
    occ_col,
    sendbuf,
    recvbuf,
    ready,
    z_send,
    z_recv,
    d_send,
    d_recv,
    f_send,
    f_recv,
    o_send,
    o_recv,
    pair_send,
    pair_recv,
    load_amps,
    load_own,
    load_rest,
):
    groups, blocks_here, vec, nij, nab, nef = dims
    rows = vec * nij
    half = rows // 2
    tail = nef % LANES
    main = nef - tail
    bulk = main // LANES * rows
    chunk = bulk + half
    cut = chunk // 32 * 16
    z = lax.axis_index("grp")
    dev = lax.axis_index("dev")
    core = dev % 2
    chip = dev // 2
    flip_x = chip + 1 - 2 * (chip % 2)
    flip_y = chip + 2 - 4 * (chip // 2)
    diag = 3 - chip
    mesh_id = pl.DeviceIdType.MESH

    def at(zz, pp, cc):
        return (zz, pp * 2 + cc)

    low = z < groups // 2

    def far(step):
        down = groups - 1 - step
        down = down - jnp.where(down <= z, 1, 0)
        up = step + jnp.where(step >= z, 1, 0)
        return jnp.where(low, down, up)

    def across(step):
        return jnp.where(low, groups // 2 + step, groups // 2 - 1 - step)

    def reach(step):
        return jnp.where(step < z, z - 1 - step, step + 1)

    loads = []
    for b in range(blocks_here):
        loads.append(pltpu.make_async_copy(amps_hbm.at[z * blocks_here + b], amps.at[b], load_amps.at[0]))
    for s in range(groups - 1):
        for b in range(blocks_here):
            slot = (s + 1) * blocks_here + b
            loads.append(
                pltpu.make_async_copy(amps_hbm.at[reach(s) * blocks_here + b], amps.at[slot], load_amps.at[1])
            )

    def bulk_parts(block, piece):
        for i in range(main // LANES):
            yield amps_hbm.at[block, :, i * LANES : (i + 1) * LANES], piece.at[i * rows : (i + 1) * rows]

    for b in range(blocks_here):
        for src, dst in bulk_parts(z * blocks_here + b, gath.at[b, z, chip]):
            loads.append(pltpu.make_async_copy(src, dst, load_own.at[0]))
    pairs = [(ints_hbm, ints), (occ_e_hbm, occ_e), (virt_e_hbm, virt_e), (vpairs_hbm, vpairs), (opairs_hbm, opairs)]
    rest = [pltpu.make_async_copy(src, dst, load_rest.at[i]) for i, (src, dst) in enumerate(pairs)]

    partner = at(z, chip, 1 - core)
    x_peer = at(z, flip_x, core)
    y_peer = at(z, flip_y, core)
    swap = chip == 2
    ways = [
        at(z, jnp.where(swap, flip_y, flip_x), core),
        at(z, jnp.where(swap, flip_x, flip_y), core),
    ]
    peers = [(partner, core == 0, 0), (x_peer, chip % 2 == 0, 1), (y_peer, chip < 2, 2)]
    last = 3 + 2 * (groups - 1)
    for s in range(groups - 1):
        zz = reach(s)
        for c in range(2):
            peers.append((at(zz, chip, core if c == 0 else 1 - core), zz > z, 3 + s * 2 + c))
    d_peer = at(z, diag, core)
    peers.append((d_peer, chip < 2, last))
    barrier = pltpu.get_barrier_semaphore()
    for peer, higher, _ in peers:
        @pl.when(higher)
        def _(peer=peer):
            pl.semaphore_signal(barrier, inc=1, device_id=peer, device_id_type=mesh_id)
    for load in loads + rest:
        load.start()
    earlier = 2 * z + chip + core

    @pl.when(earlier > 0)
    def _():
        pl.semaphore_wait(barrier, earlier)

    for i, (peer, higher, slot) in enumerate(peers):
        if i < 3 or slot == last:
            there = slot
        else:
            s, c = (i - 3) // 2, (i - 3) % 2
            zz = reach(s)
            there = 3 + c + 2 * jnp.where(z < zz, zz - 1 - z, z - 1)

        @pl.when(jnp.logical_not(higher))
        def _(peer=peer, there=there):
            pl.semaphore_signal(ready.at[there], inc=1, device_id=peer, device_id_type=mesh_id)

    def met_z(name):
        spot = outlets[name][1]
        higher = outlets[name][0] > z

        @pl.when(higher)
        def _():
            pl.semaphore_wait(ready.at[3 + 2 * spot], 1)

    def met(i):
        @pl.when(peers[i][1])
        def _():
            pl.semaphore_wait(ready.at[peers[i][2]], 1)

    def met_way(way):
        i = jnp.where(swap, 2 - way, 1 + way)
        higher = jnp.where(i == 1, chip % 2 == 0, chip < 2)

        @pl.when(higher)
        def _():
            pl.semaphore_wait(ready.at[i], 1)

    def send(src, dst, ssem, rsem, to):
        pltpu.make_async_remote_copy(
            src_ref=src, dst_ref=dst, send_sem=ssem, recv_sem=rsem, device_id=to, device_id_type=mesh_id
        ).start()

    def whole(ref, sem):
        return pltpu.make_async_remote_copy(
            src_ref=ref, dst_ref=ref, send_sem=sem, recv_sem=sem, device_id=partner, device_id_type=mesh_id
        )

    def arrived(ref, sem):
        whole(ref, sem).wait_recv()

    def left(ref, sem):
        whole(ref, sem).wait_send()

    near = z + 1 - 2 * (z % 2)
    inner = jnp.logical_and(z > 0, z < groups - 1)
    sources = {"O": (z, z), "N": (near, near), "C": (across(0),) * 2, "D": (across(1),) * 2}
    turn = [
        jnp.where(jnp.logical_or(z == groups - 1, jnp.logical_and(core == 0, z != 1)), 1, 0),
        jnp.where(jnp.logical_and(core == 1, z == 1), 0, 1),
    ]
    sources["E"] = tuple(across(t) for t in turn)
    sources["G"] = tuple(across(1 - t) for t in turn)

    def direct_main(b, way):
        for src, dst in bulk_parts(z * blocks_here + b, gath.at[b, z, chip]):
            send(src, dst, d_send.at[0], d_recv.at[b, z], ways[way])

    def direct_tail(b, way):
        send(tails.at[b], gath.at[b, z, chip, bulk:chunk], d_send.at[0], d_recv.at[b, z], ways[way])

    skip = jnp.where(z == 2, 0, 1)
    outlets = {"N": (near, 2 * (1 - skip)), "C": (across(0), skip), "D": (across(1), skip + 1)}

    def inward_main(name, b):
        to = outlets[name][0]
        for src, dst in bulk_parts(to * blocks_here + b, gath.at[b, z, chip]):
            send(src, dst, z_send.at[0], z_recv.at[b, z], at(to, chip, core))

    def inward_tail(name, b):
        to, spot = outlets[name]
        send(
            tails.at[(spot + 1) * blocks_here + b], gath.at[b, z, chip, bulk:chunk],
            z_send.at[0], z_recv.at[b, z], at(to, chip, core),
        )

    def first(name, b):
        zz = sources[name][b]
        piece = gath.at[b, zz, chip]
        arrived(piece, z_recv.at[b, zz])
        for peer in (x_peer, y_peer):
            send(piece, piece, d_send.at[0], d_recv.at[b, zz], peer)

    def second(name, b):
        zz = sources[name][b]
        arrived(gath.at[b, zz, 0:2], d_recv.at[b, zz])
        src = gath.at[b, zz, flip_x, 0:cut]
        send(src, src, f_send.at[0], f_recv.at[b], y_peer)
        src = gath.at[b, zz, flip_y, cut:chunk]
        send(src, src, f_send.at[0], f_recv.at[b], x_peer)

    def cross(name, b):
        piece = gath.at[b, sources[name][b], chip]
        send(piece, piece, f_send.at[0], f_recv.at[b], d_peer)

    def settled(name, b):
        arrived(gath.at[b, sources[name][b], 0:2], d_recv.at[b, sources[name][b]])

    def third(b):
        arrived(gath.at[b, :, diag], f_recv.at[b])

    def pack(slot):
        lower = amps[slot, 0:half, main:nef].astype(F32)
        upper = amps[slot, half:rows, main:nef].astype(F32)
        tails[slot] = jnp.concatenate([lower, upper], axis=1).astype(BF16)

    def loaded(slots, sem):
        pltpu.make_async_copy(amps.at[slots], amps.at[slots], sem).wait()


    @pl.when(chip == 3)
    def _():
        met_way(0)
        direct_main(0, 0)
        met_way(1)
        direct_main(0, 1)

        @pl.when(jnp.logical_not(inner))
        def _():
            met_z("N")
            inward_main("N", 0)

        loaded(slice(0, blocks_here), load_amps.at[0])
        for b in range(blocks_here):
            pack(b)
        direct_tail(0, 0)
        direct_tail(0, 1)
        direct_main(1, 0)
        direct_main(1, 1)
        direct_tail(1, 0)
        direct_tail(1, 1)
        loaded(slice(blocks_here, groups * blocks_here), load_amps.at[1])
        for slot in range(blocks_here, groups * blocks_here):
            pack(slot)

    @pl.when(jnp.logical_not(chip == 3))
    def _():

        @pl.when(jnp.logical_not(chip == 0))
        def _():
            met_way(0)
            direct_main(0, 0)


        @pl.when(jnp.logical_not(inner))
        def _():
            met_z("N")
            inward_main("N", 0)

        loaded(slice(0, blocks_here), load_amps.at[0])
        for b in range(blocks_here):
            pack(b)
        loaded(slice(blocks_here, groups * blocks_here), load_amps.at[1])
        for slot in range(blocks_here, groups * blocks_here):
            pack(slot)

        @pl.when(chip == 0)
        def _():
            met_way(0)
            direct_main(0, 0)


        @pl.when(jnp.logical_not(inner))
        def _():
            inward_tail("N", 0)

        direct_tail(0, 0)
        direct_main(1, 0)
        direct_tail(1, 0)

        @pl.when(inner)
        def _():

            @pl.when(z == 2)
            def _():

                @pl.when(core == 0)
                def _():
                    met_z("C")
                    inward_main("C", 0)
                    inward_tail("C", 0)
                    met_z("D")
                    inward_main("D", 0)
                    inward_tail("D", 0)
                    met_z("N")
                    inward_main("N", 0)
                    inward_tail("N", 0)
                    inward_main("C", 1)
                    inward_tail("C", 1)
                    inward_main("D", 1)
                    inward_tail("D", 1)
                    inward_main("N", 1)
                    inward_tail("N", 1)

                @pl.when(jnp.logical_not(core == 0))
                def _():
                    met_z("C")
                    inward_main("C", 0)
                    inward_tail("C", 0)
                    met_z("D")
                    inward_main("D", 0)
                    inward_tail("D", 0)
                    met_z("N")
                    inward_main("N", 0)
                    inward_tail("N", 0)
                    inward_main("C", 1)
                    inward_tail("C", 1)
                    inward_main("D", 1)
                    inward_tail("D", 1)
                    inward_main("N", 1)
                    inward_tail("N", 1)


            @pl.when(jnp.logical_not(z == 2))
            def _():

                @pl.when(core == 0)
                def _():
                    met_z("N")
                    inward_main("N", 0)
                    inward_tail("N", 0)
                    met_z("C")
                    inward_main("C", 0)
                    inward_tail("C", 0)
                    met_z("D")
                    inward_main("D", 0)
                    inward_tail("D", 0)
                    inward_main("N", 1)
                    inward_tail("N", 1)
                    inward_main("C", 1)
                    inward_tail("C", 1)
                    inward_main("D", 1)
                    inward_tail("D", 1)

                @pl.when(jnp.logical_not(core == 0))
                def _():
                    met_z("N")
                    inward_main("N", 0)
                    inward_tail("N", 0)
                    met_z("C")
                    inward_main("C", 0)
                    inward_tail("C", 0)
                    met_z("D")
                    inward_main("D", 0)
                    inward_tail("D", 0)
                    inward_main("N", 1)
                    inward_tail("N", 1)
                    inward_main("C", 1)
                    inward_tail("C", 1)
                    inward_main("D", 1)
                    inward_tail("D", 1)


        @pl.when(jnp.logical_not(inner))
        def _():
            met_z("C")
            inward_main("C", 0)
            inward_tail("C", 0)

        met_way(1)
        direct_main(0, 1)
        direct_tail(0, 1)
        direct_main(1, 1)
        direct_tail(1, 1)


    @pl.when(chip == 3)
    def _():

        @pl.when(inner)
        def _():

            @pl.when(z == 2)
            def _():

                @pl.when(core == 0)
                def _():
                    met_z("C")
                    inward_main("C", 0)
                    inward_tail("C", 0)
                    met_z("D")
                    inward_main("D", 0)
                    inward_tail("D", 0)
                    met_z("N")
                    inward_main("N", 0)
                    inward_tail("N", 0)
                    inward_main("C", 1)
                    inward_tail("C", 1)
                    inward_main("D", 1)
                    inward_tail("D", 1)
                    inward_main("N", 1)
                    inward_tail("N", 1)

                @pl.when(jnp.logical_not(core == 0))
                def _():
                    met_z("C")
                    inward_main("C", 0)
                    inward_tail("C", 0)
                    met_z("D")
                    inward_main("D", 0)
                    inward_tail("D", 0)
                    met_z("N")
                    inward_main("N", 0)
                    inward_tail("N", 0)
                    inward_main("C", 1)
                    inward_tail("C", 1)
                    inward_main("D", 1)
                    inward_tail("D", 1)
                    inward_main("N", 1)
                    inward_tail("N", 1)


            @pl.when(jnp.logical_not(z == 2))
            def _():

                @pl.when(core == 0)
                def _():
                    met_z("N")
                    inward_main("N", 0)
                    inward_tail("N", 0)
                    met_z("C")
                    inward_main("C", 0)
                    inward_tail("C", 0)
                    met_z("D")
                    inward_main("D", 0)
                    inward_tail("D", 0)
                    inward_main("N", 1)
                    inward_tail("N", 1)
                    inward_main("C", 1)
                    inward_tail("C", 1)
                    inward_main("D", 1)
                    inward_tail("D", 1)

                @pl.when(jnp.logical_not(core == 0))
                def _():
                    met_z("N")
                    inward_main("N", 0)
                    inward_tail("N", 0)
                    met_z("C")
                    inward_main("C", 0)
                    inward_tail("C", 0)
                    met_z("D")
                    inward_main("D", 0)
                    inward_tail("D", 0)
                    inward_main("N", 1)
                    inward_tail("N", 1)
                    inward_main("C", 1)
                    inward_tail("C", 1)
                    inward_main("D", 1)
                    inward_tail("D", 1)


        @pl.when(jnp.logical_not(inner))
        def _():
            inward_tail("N", 0)
            met_z("C")
            inward_main("C", 0)
            inward_tail("C", 0)
            met_z("D")
            inward_main("D", 0)
            inward_tail("D", 0)
            inward_main("N", 1)
            inward_tail("N", 1)
            inward_main("C", 1)
            inward_tail("C", 1)
            inward_main("D", 1)
            inward_tail("D", 1)


    @pl.when(jnp.logical_not(chip == 3))
    def _():

        @pl.when(jnp.logical_not(inner))
        def _():
            met_z("D")
            inward_main("D", 0)
            inward_tail("D", 0)
            inward_main("N", 1)
            inward_tail("N", 1)
            inward_main("C", 1)
            inward_tail("C", 1)
            inward_main("D", 1)
            inward_tail("D", 1)


    met(0)
    send(vpairs_hbm, other_pairs, pair_send.at[0], pair_recv.at[0], partner)
    send(ints_hbm, other_ints, pair_send.at[1], pair_recv.at[1], partner)
    for b in range(blocks_here):
        gath[b, z, chip, bulk:chunk] = tails[b]
    for load in rest:
        load.wait()

    occ_column = as_column(occ_e[...].reshape(1, -1))
    occ_row = picked_row(occ_column, opairs[0:1, :]) + picked_row(occ_column, opairs[1:2, :])
    occ_col[...] = jnp.broadcast_to(as_column(occ_row), occ_col.shape)
    virt_column = as_column(virt_e[...].reshape(1, -1))

    def prepare(side, int_ref, pair_ref):
        for b in range(blocks_here):
            virt_row = picked_row(virt_column, pair_ref[b, 0:1, :]) + picked_row(
                virt_column, pair_ref[b, 1:2, :]
            )
            for p in range(gath.shape[2]):
                start = pl.multiple_of((2 * p + core) * nij, 8)
                occ = occ_col[pl.ds(start, nij), 0:1]
                recip[b, side, p] = 1.0 / (occ - virt_row)
            for zz in range(groups):
                panel = int_ref[b, :, zz * nef : (zz + 1) * nef].astype(F32)
                last = panel[:, main:nef]
                wide = jnp.concatenate([panel[:, 0:main], last, last], axis=1)
                width = main + LANES
                weights[b, side, :, zz * width : (zz + 1) * width] = wide.astype(BF16)

    lane = lax.broadcasted_iota(jnp.int32, (half, LANES), 1)
    main_lanes = nab // LANES * LANES

    def job(b, p):
        parts = []
        for zz in range(groups):
            end = gath[b, zz, p, bulk:chunk]
            zero = jnp.zeros_like(end)
            end2 = jnp.concatenate(
                [jnp.where(lane < tail, end, zero), jnp.where(lane < tail, zero, end)], axis=0
            )
            parts += [gath[b, zz, p, i * rows : (i + 1) * rows] for i in range(main // LANES)] + [end2]
        panel = jnp.concatenate(parts, axis=1)
        for side in range(2):
            total = lax.dot_general(
                panel, weights[b, side], (((1,), (1,)), ((), ())), preferred_element_type=F32
            )
            scaled = total.reshape(vec, nij, nab) * recip[b, side, p][None]
            ends = [scaled[v, :, main_lanes:nab] for v in range(vec)]
            sendbuf[b, p, side, 0:rows, :] = scaled[:, :, 0:main_lanes].reshape(rows, main_lanes).astype(BF16)
            sendbuf[b, p, side, rows : rows + nij, :] = jnp.concatenate(ends, axis=1).astype(BF16)

        @pl.when(p != z)
        def _():
            for side in range(2):
                send(
                    sendbuf.at[b, p, side], recvbuf.at[z, b, core], o_send.at[0], o_recv.at[z, b],
                    at(p, chip, core if side == 0 else 1 - core),
                )

        @pl.when(p == z)
        def _():
            send(sendbuf.at[b, z, 1], recvbuf.at[z, b, core], o_send.at[1], o_recv.at[z, b], partner)
            recvbuf[z, b, core] = sendbuf[b, z, 0]

    wanted = [far(s) for s in range(groups - 1)] + [z]
    spot = sum(jnp.where(wanted[i] == diag, i, 0) for i in range(groups))
    late = [jnp.where(i >= spot, wanted[i + 1], wanted[i]) for i in range(groups - 1)] + [diag]

    def unpack(zz, b):
        got = [recvbuf[zz, b, c].astype(F32) for c in range(2)]
        width = nab - main_lanes
        for v in range(vec):
            pieces = []
            for c in range(2):
                body_rows = got[c][v * nij : (v + 1) * nij, :]
                end = got[c][rows : rows + nij, v * width : (v + 1) * width]
                pieces.append(jnp.concatenate([body_rows, end], axis=1))
            out[zz * blocks_here + b, v] = jnp.concatenate(pieces, axis=0).astype(BF16)

    prepare(0, ints, vpairs)
    second("O", 0)
    first("N", 0)
    second("O", 1)
    arrived(other_pairs, pair_recv.at[0])
    arrived(other_ints, pair_recv.at[1])
    prepare(1, other_ints, other_pairs)

    @pl.when(inner)
    def _():
        first("E", 0)
        first("G", 0)
        second("N", 0)
        first("N", 1)
        second("E", 0)
        first("E", 1)
        second("G", 0)

    @pl.when(jnp.logical_not(inner))
    def _():
        first("N", 1)
        second("N", 0)
        second("N", 1)
        first("E", 0)
        first("G", 0)
        second("E", 0)
        first("E", 1)
        second("G", 0)

    met(len(peers) - 1)
    first("G", 1)
    cross("G", 1)
    pltpu.make_async_copy(gath.at[:, z, chip, 0:bulk], gath.at[:, z, chip, 0:bulk], load_own.at[0]).wait()
    for s in range(groups - 1):
        met(4 + 2 * s)

    @pl.when(inner)
    def _():
        second("N", 1)

    job(0, late[0])
    job(0, late[1])
    second("E", 1)
    job(0, late[2])
    third(0)
    job(0, late[3])
    settled("G", 1)
    job(1, late[0])
    job(1, late[1])
    job(1, late[2])
    third(1)
    job(1, late[3])

    for b in range(blocks_here):
        arrived(recvbuf.at[z, b, 1 - core], o_recv.at[z, b])
        unpack(z, b)
        for s in range(groups - 1):
            zz = far(s)
            arrived(recvbuf.at[zz, b], o_recv.at[zz, b])
            unpack(zz, b)
    left(gath.at[:, 0 : groups - 1, 0], z_send.at[0])
    left(gath.at[0], d_send.at[0])
    left(gath.at[:, :, 0], f_send.at[0])
    left(sendbuf.at[:, 0 : groups - 1], o_send.at[0])
    left(sendbuf.at[:, 0, 0], o_send.at[1])
    left(other_pairs, pair_send.at[0])
    left(other_ints, pair_send.at[1])


def fused(groups, integrals, amplitudes, occupied_energy, virtual_energy, virtual_pairs, occupied_pairs):
    nblk, nef, vec, nij = amplitudes.shape
    here, nab, _ = integrals.shape
    rows = vec * nij
    chips = lax.axis_size("dev") // 2
    amps = jnp.transpose(amplitudes, (0, 2, 3, 1)).reshape(nblk, rows, nef)
    vpairs = jnp.transpose(virtual_pairs, (0, 2, 1))
    opairs = jnp.transpose(occupied_pairs, (1, 0))
    dims = (groups, here, vec, nij, nab, nef)
    dma = pltpu.SemaphoreType.DMA
    arrays = (integrals, amps, occupied_energy, virtual_energy, vpairs, opairs)
    result = pl.pallas_call(
        functools.partial(body, dims),
        out_shape=jax.ShapeDtypeStruct((nblk, vec, 2 * nij, nab), BF16),
        in_specs=[pl.BlockSpec(memory_space=pltpu.HBM)] * 6,
        out_specs=pl.BlockSpec(memory_space=pltpu.VMEM),
        scratch_shapes=[
            pltpu.VMEM(integrals.shape, BF16),
            pltpu.VMEM(amps.shape, BF16),
            pltpu.VMEM(occupied_energy.shape, F32),
            pltpu.VMEM(virtual_energy.shape, F32),
            pltpu.VMEM(vpairs.shape, jnp.int32),
            pltpu.VMEM(opairs.shape, jnp.int32),
            pltpu.VMEM((nblk, rows // 2, LANES), BF16),
            pltpu.VMEM((here, groups, chips, 2 * rows + rows // 2, LANES), BF16),
            pltpu.VMEM(integrals.shape, BF16),
            pltpu.VMEM(vpairs.shape, jnp.int32),
            pltpu.VMEM((here, 2, nab, groups * 3 * LANES), BF16),
            pltpu.VMEM((here, 2, chips, nij, nab), F32),
            pltpu.VMEM((2 * chips * nij, LANES), F32),
            pltpu.VMEM((here, groups, 2, rows + nij, LANES), BF16),
            pltpu.VMEM((groups, here, 2, rows + nij, LANES), BF16),
            pltpu.SemaphoreType.REGULAR((4 + 2 * (groups - 1),)),
            dma((1,)),
            dma((here, groups)),
            dma((1,)),
            dma((here, groups)),
            dma((1,)),
            dma((here,)),
            dma((2,)),
            dma((groups, here)),
            dma((2,)),
            dma((2,)),
            dma((2,)),
            dma((1,)),
            dma((5,)),
        ],
        compiler_params=pltpu.CompilerParams(
            collective_id=0, has_side_effects=True, vmem_limit_bytes=32 * 1024 * 1024
        ),
        name="ladder",
    )(*[pltpu.with_memory_space_constraint(array, pltpu.HBM) for array in arrays])
    return jnp.transpose(result, (0, 3, 1, 2))


def solution(mesh):
    placed = (
        P("grp", "dev", None),
        P(None, "grp", None, "dev"),
        P(),
        P(),
        P("grp", "dev", None),
        P(),
    )
    groups, devs = mesh.shape["grp"], mesh.shape["dev"]

    def local(integrals, amplitudes, *rest):
        nef, vec, nij = amplitudes.shape[1:]
        nab = integrals.shape[1]
        square = devs == 2 * 2 * 2 and devs == 2 * groups
        packs = (
            2 * LANES < nef < 3 * LANES
            and 2 * (nef % LANES) == LANES
            and LANES < nab < 2 * LANES
            and vec * (nab % LANES) == LANES
            and nij % 8 == 0
            and (vec * nij) % 32 == 0
        )
        if square and packs:
            return fused(groups, integrals, amplitudes, *rest)
        return plain(integrals, amplitudes, *rest)

    return jax.shard_map(
        local, mesh=mesh, in_specs=placed, out_specs=P(None, "dev", None, "grp"), check_vma=False
    )
```

```python
import functools

import jax
import jax.numpy as jnp
from jax import lax
from jax.experimental import pallas as pl
from jax.experimental.pallas import tpu as pltpu
from jax.sharding import PartitionSpec as P

LANES = 128
F32 = jnp.float32
BF16 = jnp.bfloat16


def lookup(energy, indices):
    labels = jnp.arange(energy.shape[0], dtype=jnp.int32)
    picked = indices[:, None] == labels[None, :]
    return jnp.sum(jnp.where(picked, energy[None, :], 0.0), axis=1)


def plain(integrals, amplitudes, occupied_energy, virtual_energy, virtual_pairs, occupied_pairs):
    arrived = lax.all_to_all(amplitudes, "grp", split_axis=0, concat_axis=1, tiled=True)
    occ_sum = lookup(occupied_energy, occupied_pairs[:, 0]) + lookup(
        occupied_energy, occupied_pairs[:, 1]
    )
    results = []
    for block in range(arrived.shape[0]):
        panel = arrived[block]
        block_ints = integrals[block]
        gathered = lax.all_gather(panel, "dev", axis=2, tiled=True)
        ladder = jnp.einsum("ae,evj->avj", block_ints, gathered, preferred_element_type=jnp.float32)
        pairs_here = virtual_pairs[block]
        virt_sum = lookup(virtual_energy, pairs_here[:, 0]) + lookup(
            virtual_energy, pairs_here[:, 1]
        )
        denominator = occ_sum[None, :] - virt_sum[:, None]
        results.append((ladder / denominator[:, None, :]).astype(jnp.bfloat16))
    stacked = jnp.stack(results)
    return lax.all_to_all(stacked, "grp", split_axis=3, concat_axis=0, tiled=True)


def as_column(row):
    n = row.shape[1]
    eye = lax.broadcasted_iota(jnp.int32, (n, n), 0) == lax.broadcasted_iota(jnp.int32, (n, n), 1)
    return jnp.sum(jnp.where(eye, jnp.broadcast_to(row, (n, n)), 0.0), axis=1, keepdims=True)


def picked_row(column, index_row):
    shape = (column.shape[0], index_row.shape[1])
    hit = lax.broadcasted_iota(jnp.int32, shape, 0) == jnp.broadcast_to(index_row, shape)
    return jnp.sum(jnp.where(hit, jnp.broadcast_to(column, shape), 0.0), axis=0, keepdims=True)


def body(
    dims,
    ints_hbm,
    amps_hbm,
    occ_e_hbm,
    virt_e_hbm,
    vpairs_hbm,
    opairs_hbm,
    out,
    ints,
    amps,
    occ_e,
    virt_e,
    vpairs,
    opairs,
    tails,
    gath,
    other_ints,
    other_pairs,
    weights,
    recip,
    occ_col,
    sendbuf,
    recvbuf,
    ready,
    z_send,
    z_recv,
    d_send,
    d_recv,
    f_send,
    f_recv,
    o_send,
    o_recv,
    pair_send,
    pair_recv,
    load_amps,
    load_own,
    load_rest,
):
    groups, blocks_here, vec, nij, nab, nef = dims
    rows = vec * nij
    half = rows // 2
    tail = nef % LANES
    main = nef - tail
    bulk = main // LANES * rows
    chunk = bulk + half
    cut = chunk // 32 * 16
    z = lax.axis_index("grp")
    dev = lax.axis_index("dev")
    core = dev % 2
    chip = dev // 2
    flip_x = chip + 1 - 2 * (chip % 2)
    flip_y = chip + 2 - 4 * (chip // 2)
    diag = 3 - chip
    mesh_id = pl.DeviceIdType.MESH

    def at(zz, pp, cc):
        return (zz, pp * 2 + cc)

    low = z < groups // 2

    def far(step):
        down = groups - 1 - step
        down = down - jnp.where(down <= z, 1, 0)
        up = step + jnp.where(step >= z, 1, 0)
        return jnp.where(low, down, up)

    def across(step):
        return jnp.where(low, groups // 2 + step, groups // 2 - 1 - step)

    def reach(step):
        return jnp.where(step < z, z - 1 - step, step + 1)

    loads = []
    for b in range(blocks_here):
        loads.append(pltpu.make_async_copy(amps_hbm.at[z * blocks_here + b], amps.at[b], load_amps.at[0]))
    for s in range(groups - 1):
        for b in range(blocks_here):
            slot = (s + 1) * blocks_here + b
            loads.append(
                pltpu.make_async_copy(amps_hbm.at[reach(s) * blocks_here + b], amps.at[slot], load_amps.at[1])
            )

    def bulk_parts(block, piece):
        for i in range(main // LANES):
            yield amps_hbm.at[block, :, i * LANES : (i + 1) * LANES], piece.at[i * rows : (i + 1) * rows]

    for b in range(blocks_here):
        for src, dst in bulk_parts(z * blocks_here + b, gath.at[b, z, chip]):
            loads.append(pltpu.make_async_copy(src, dst, load_own.at[0]))
    pairs = [(ints_hbm, ints), (occ_e_hbm, occ_e), (virt_e_hbm, virt_e), (vpairs_hbm, vpairs), (opairs_hbm, opairs)]
    rest = [pltpu.make_async_copy(src, dst, load_rest.at[i]) for i, (src, dst) in enumerate(pairs)]

    partner = at(z, chip, 1 - core)
    x_peer = at(z, flip_x, core)
    y_peer = at(z, flip_y, core)
    swap = chip == 2
    ways = [
        at(z, jnp.where(swap, flip_y, flip_x), core),
        at(z, jnp.where(swap, flip_x, flip_y), core),
    ]
    peers = [(partner, core == 0, 0), (x_peer, chip % 2 == 0, 1), (y_peer, chip < 2, 2)]
    last = 3 + 2 * (groups - 1)
    for s in range(groups - 1):
        zz = reach(s)
        for c in range(2):
            peers.append((at(zz, chip, core if c == 0 else 1 - core), zz > z, 3 + s * 2 + c))
    d_peer = at(z, diag, core)
    peers.append((d_peer, chip < 2, last))
    barrier = pltpu.get_barrier_semaphore()
    for peer, higher, _ in peers:
        @pl.when(higher)
        def _(peer=peer):
            pl.semaphore_signal(barrier, inc=1, device_id=peer, device_id_type=mesh_id)
    for load in loads + rest:
        load.start()
    earlier = 2 * z + chip + core

    @pl.when(earlier > 0)
    def _():
        pl.semaphore_wait(barrier, earlier)

    for i, (peer, higher, slot) in enumerate(peers):
        if i < 3 or slot == last:
            there = slot
        else:
            s, c = (i - 3) // 2, (i - 3) % 2
            zz = reach(s)
            there = 3 + c + 2 * jnp.where(z < zz, zz - 1 - z, z - 1)

        @pl.when(jnp.logical_not(higher))
        def _(peer=peer, there=there):
            pl.semaphore_signal(ready.at[there], inc=1, device_id=peer, device_id_type=mesh_id)

    def met_z(name):
        spot = outlets[name][1]
        higher = outlets[name][0] > z

        @pl.when(higher)
        def _():
            pl.semaphore_wait(ready.at[3 + 2 * spot], 1)

    def met(i):
        @pl.when(peers[i][1])
        def _():
            pl.semaphore_wait(ready.at[peers[i][2]], 1)

    def met_way(way):
        i = jnp.where(swap, 2 - way, 1 + way)
        higher = jnp.where(i == 1, chip % 2 == 0, chip < 2)

        @pl.when(higher)
        def _():
            pl.semaphore_wait(ready.at[i], 1)

    def send(src, dst, ssem, rsem, to):
        pltpu.make_async_remote_copy(
            src_ref=src, dst_ref=dst, send_sem=ssem, recv_sem=rsem, device_id=to, device_id_type=mesh_id
        ).start()

    def whole(ref, sem):
        return pltpu.make_async_remote_copy(
            src_ref=ref, dst_ref=ref, send_sem=sem, recv_sem=sem, device_id=partner, device_id_type=mesh_id
        )

    def arrived(ref, sem):
        whole(ref, sem).wait_recv()

    def left(ref, sem):
        whole(ref, sem).wait_send()

    near = z + 1 - 2 * (z % 2)
    inner = jnp.logical_and(z > 0, z < groups - 1)
    sources = {"O": (z, z), "N": (near, near), "C": (across(0),) * 2, "D": (across(1),) * 2}
    turn = [
        jnp.where(jnp.logical_or(z == groups - 1, jnp.logical_and(core == 0, z != 1)), 1, 0),
        jnp.where(jnp.logical_and(core == 1, z == 1), 0, 1),
    ]
    sources["E"] = tuple(across(t) for t in turn)
    sources["G"] = tuple(across(1 - t) for t in turn)

    def direct_main(b, way):
        for src, dst in bulk_parts(z * blocks_here + b, gath.at[b, z, chip]):
            send(src, dst, d_send.at[0], d_recv.at[b, z], ways[way])

    def direct_tail(b, way):
        send(tails.at[b], gath.at[b, z, chip, bulk:chunk], d_send.at[0], d_recv.at[b, z], ways[way])

    skip = jnp.where(z == 2, 0, 1)
    outlets = {"N": (near, 2 * (1 - skip)), "C": (across(0), skip), "D": (across(1), skip + 1)}

    def inward_main(name, b):
        to = outlets[name][0]
        for src, dst in bulk_parts(to * blocks_here + b, gath.at[b, z, chip]):
            send(src, dst, z_send.at[0], z_recv.at[b, z], at(to, chip, core))

    def inward_tail(name, b):
        to, spot = outlets[name]
        send(
            tails.at[(spot + 1) * blocks_here + b], gath.at[b, z, chip, bulk:chunk],
            z_send.at[0], z_recv.at[b, z], at(to, chip, core),
        )

    def first(name, b):
        zz = sources[name][b]
        piece = gath.at[b, zz, chip]
        arrived(piece, z_recv.at[b, zz])
        for peer in (x_peer, y_peer):
            send(piece, piece, d_send.at[0], d_recv.at[b, zz], peer)

    def second(name, b):
        zz = sources[name][b]
        arrived(gath.at[b, zz, 0:2], d_recv.at[b, zz])
        src = gath.at[b, zz, flip_x, 0:cut]
        send(src, src, f_send.at[0], f_recv.at[b], y_peer)
        src = gath.at[b, zz, flip_y, cut:chunk]
        send(src, src, f_send.at[0], f_recv.at[b], x_peer)

    def cross(name, b):
        piece = gath.at[b, sources[name][b], chip]
        send(piece, piece, f_send.at[0], f_recv.at[b], d_peer)

    def settled(name, b):
        arrived(gath.at[b, sources[name][b], 0:2], d_recv.at[b, sources[name][b]])

    def third(b):
        arrived(gath.at[b, :, diag], f_recv.at[b])

    def pack(slot):
        lower = amps[slot, 0:half, main:nef].astype(F32)
        upper = amps[slot, half:rows, main:nef].astype(F32)
        tails[slot] = jnp.concatenate([lower, upper], axis=1).astype(BF16)

    def loaded(slots, sem):
        pltpu.make_async_copy(amps.at[slots], amps.at[slots], sem).wait()


    @pl.when(chip == 3)
    def _():
        met_way(0)
        direct_main(0, 0)
        met_way(1)
        direct_main(0, 1)

        @pl.when(jnp.logical_not(inner))
        def _():
            met_z("N")
            inward_main("N", 0)

        loaded(slice(0, blocks_here), load_amps.at[0])
        for b in range(blocks_here):
            pack(b)
        direct_tail(0, 0)
        direct_tail(0, 1)
        direct_main(1, 0)
        direct_main(1, 1)
        direct_tail(1, 0)
        direct_tail(1, 1)
        loaded(slice(blocks_here, groups * blocks_here), load_amps.at[1])
        for slot in range(blocks_here, groups * blocks_here):
            pack(slot)

    @pl.when(jnp.logical_not(chip == 3))
    def _():

        @pl.when(jnp.logical_not(chip == 0))
        def _():
            met_way(0)
            direct_main(0, 0)


        @pl.when(jnp.logical_not(inner))
        def _():
            met_z("N")
            inward_main("N", 0)

        loaded(slice(0, blocks_here), load_amps.at[0])
        for b in range(blocks_here):
            pack(b)
        loaded(slice(blocks_here, groups * blocks_here), load_amps.at[1])
        for slot in range(blocks_here, groups * blocks_here):
            pack(slot)

        @pl.when(chip == 0)
        def _():
            met_way(0)
            direct_main(0, 0)


        @pl.when(jnp.logical_not(inner))
        def _():
            inward_tail("N", 0)

        direct_tail(0, 0)
        direct_main(1, 0)
        direct_tail(1, 0)

        @pl.when(inner)
        def _():

            @pl.when(z == 2)
            def _():

                @pl.when(core == 0)
                def _():
                    met_z("C")
                    inward_main("C", 0)
                    inward_tail("C", 0)
                    met_z("D")
                    inward_main("D", 0)
                    inward_tail("D", 0)
                    met_z("N")
                    inward_main("N", 0)
                    inward_tail("N", 0)
                    inward_main("C", 1)
                    inward_tail("C", 1)
                    inward_main("D", 1)
                    inward_tail("D", 1)
                    inward_main("N", 1)
                    inward_tail("N", 1)

                @pl.when(jnp.logical_not(core == 0))
                def _():
                    met_z("C")
                    inward_main("C", 0)
                    inward_tail("C", 0)
                    met_z("D")
                    inward_main("D", 0)
                    inward_tail("D", 0)
                    met_z("N")
                    inward_main("N", 0)
                    inward_tail("N", 0)
                    inward_main("C", 1)
                    inward_tail("C", 1)
                    inward_main("D", 1)
                    inward_tail("D", 1)
                    inward_main("N", 1)
                    inward_tail("N", 1)


            @pl.when(jnp.logical_not(z == 2))
            def _():

                @pl.when(core == 0)
                def _():
                    met_z("N")
                    inward_main("N", 0)
                    inward_tail("N", 0)
                    met_z("C")
                    inward_main("C", 0)
                    inward_tail("C", 0)
                    met_z("D")
                    inward_main("D", 0)
                    inward_tail("D", 0)
                    inward_main("N", 1)
                    inward_tail("N", 1)
                    inward_main("C", 1)
                    inward_tail("C", 1)
                    inward_main("D", 1)
                    inward_tail("D", 1)

                @pl.when(jnp.logical_not(core == 0))
                def _():
                    met_z("N")
                    inward_main("N", 0)
                    inward_tail("N", 0)
                    met_z("C")
                    inward_main("C", 0)
                    inward_tail("C", 0)
                    met_z("D")
                    inward_main("D", 0)
                    inward_tail("D", 0)
                    inward_main("N", 1)
                    inward_tail("N", 1)
                    inward_main("C", 1)
                    inward_tail("C", 1)
                    inward_main("D", 1)
                    inward_tail("D", 1)


        @pl.when(jnp.logical_not(inner))
        def _():
            met_z("C")
            inward_main("C", 0)
            inward_tail("C", 0)

        met_way(1)
        direct_main(0, 1)
        direct_tail(0, 1)
        direct_main(1, 1)
        direct_tail(1, 1)


    @pl.when(chip == 3)
    def _():

        @pl.when(inner)
        def _():

            @pl.when(z == 2)
            def _():

                @pl.when(core == 0)
                def _():
                    met_z("C")
                    inward_main("C", 0)
                    inward_tail("C", 0)
                    met_z("D")
                    inward_main("D", 0)
                    inward_tail("D", 0)
                    met_z("N")
                    inward_main("N", 0)
                    inward_tail("N", 0)
                    inward_main("C", 1)
                    inward_tail("C", 1)
                    inward_main("D", 1)
                    inward_tail("D", 1)
                    inward_main("N", 1)
                    inward_tail("N", 1)

                @pl.when(jnp.logical_not(core == 0))
                def _():
                    met_z("C")
                    inward_main("C", 0)
                    inward_tail("C", 0)
                    met_z("D")
                    inward_main("D", 0)
                    inward_tail("D", 0)
                    met_z("N")
                    inward_main("N", 0)
                    inward_tail("N", 0)
                    inward_main("C", 1)
                    inward_tail("C", 1)
                    inward_main("D", 1)
                    inward_tail("D", 1)
                    inward_main("N", 1)
                    inward_tail("N", 1)


            @pl.when(jnp.logical_not(z == 2))
            def _():

                @pl.when(core == 0)
                def _():
                    met_z("N")
                    inward_main("N", 0)
                    inward_tail("N", 0)
                    met_z("C")
                    inward_main("C", 0)
                    inward_tail("C", 0)
                    met_z("D")
                    inward_main("D", 0)
                    inward_tail("D", 0)
                    inward_main("N", 1)
                    inward_tail("N", 1)
                    inward_main("C", 1)
                    inward_tail("C", 1)
                    inward_main("D", 1)
                    inward_tail("D", 1)

                @pl.when(jnp.logical_not(core == 0))
                def _():
                    met_z("N")
                    inward_main("N", 0)
                    inward_tail("N", 0)
                    met_z("C")
                    inward_main("C", 0)
                    inward_tail("C", 0)
                    met_z("D")
                    inward_main("D", 0)
                    inward_tail("D", 0)
                    inward_main("N", 1)
                    inward_tail("N", 1)
                    inward_main("C", 1)
                    inward_tail("C", 1)
                    inward_main("D", 1)
                    inward_tail("D", 1)


        @pl.when(jnp.logical_not(inner))
        def _():
            inward_tail("N", 0)
            met_z("C")
            inward_main("C", 0)
            inward_tail("C", 0)
            met_z("D")
            inward_main("D", 0)
            inward_tail("D", 0)
            inward_main("N", 1)
            inward_tail("N", 1)
            inward_main("C", 1)
            inward_tail("C", 1)
            inward_main("D", 1)
            inward_tail("D", 1)


    @pl.when(jnp.logical_not(chip == 3))
    def _():

        @pl.when(jnp.logical_not(inner))
        def _():
            met_z("D")
            inward_main("D", 0)
            inward_tail("D", 0)
            inward_main("N", 1)
            inward_tail("N", 1)
            inward_main("C", 1)
            inward_tail("C", 1)
            inward_main("D", 1)
            inward_tail("D", 1)


    met(0)
    send(vpairs_hbm, other_pairs, pair_send.at[0], pair_recv.at[0], partner)
    send(ints_hbm, other_ints, pair_send.at[1], pair_recv.at[1], partner)
    for b in range(blocks_here):
        gath[b, z, chip, bulk:chunk] = tails[b]
    for load in rest:
        load.wait()

    occ_column = as_column(occ_e[...].reshape(1, -1))
    occ_row = picked_row(occ_column, opairs[0:1, :]) + picked_row(occ_column, opairs[1:2, :])
    occ_col[...] = jnp.broadcast_to(as_column(occ_row), occ_col.shape)
    virt_column = as_column(virt_e[...].reshape(1, -1))

    def prepare(side, int_ref, pair_ref):
        for b in range(blocks_here):
            virt_row = picked_row(virt_column, pair_ref[b, 0:1, :]) + picked_row(
                virt_column, pair_ref[b, 1:2, :]
            )
            for p in range(gath.shape[2]):
                start = pl.multiple_of((2 * p + core) * nij, 8)
                occ = occ_col[pl.ds(start, nij), 0:1]
                recip[b, side, p] = 1.0 / (occ - virt_row)
            for zz in range(groups):
                panel = int_ref[b, :, zz * nef : (zz + 1) * nef].astype(F32)
                last = panel[:, main:nef]
                wide = jnp.concatenate([panel[:, 0:main], last, last], axis=1)
                width = main + LANES
                weights[b, side, :, zz * width : (zz + 1) * width] = wide.astype(BF16)

    lane = lax.broadcasted_iota(jnp.int32, (half, LANES), 1)
    main_lanes = nab // LANES * LANES

    def job(b, *columns):
        panels = []
        for p in columns:
            parts = []
            for zz in range(groups):
                end = gath[b, zz, p, bulk:chunk]
                zero = jnp.zeros_like(end)
                end2 = jnp.concatenate(
                    [jnp.where(lane < tail, end, zero), jnp.where(lane < tail, zero, end)], axis=0
                )
                parts += [gath[b, zz, p, i * rows : (i + 1) * rows] for i in range(main // LANES)] + [end2]
            panels.append(jnp.concatenate(parts, axis=1))
        panel = jnp.concatenate(panels, axis=0)
        for side in range(2):
            total = lax.dot_general(
                panel, weights[b, side], (((1,), (1,)), ((), ())), preferred_element_type=F32
            )
            for i, p in enumerate(columns):
                scaled = total[i * rows : (i + 1) * rows].reshape(vec, nij, nab) * recip[b, side, p][None]
                ends = [scaled[v, :, main_lanes:nab] for v in range(vec)]
                sendbuf[b, p, side, 0:rows, :] = scaled[:, :, 0:main_lanes].reshape(rows, main_lanes).astype(BF16)
                sendbuf[b, p, side, rows : rows + nij, :] = jnp.concatenate(ends, axis=1).astype(BF16)
        for p in columns:
            deliver(b, p)

    def deliver(b, p):
        @pl.when(p != z)
        def _():
            for side in range(2):
                send(
                    sendbuf.at[b, p, side], recvbuf.at[z, b, core], o_send.at[0], o_recv.at[z, b],
                    at(p, chip, core if side == 0 else 1 - core),
                )

        @pl.when(p == z)
        def _():
            send(sendbuf.at[b, z, 1], recvbuf.at[z, b, core], o_send.at[1], o_recv.at[z, b], partner)
            recvbuf[z, b, core] = sendbuf[b, z, 0]

    wanted = [far(s) for s in range(groups - 1)] + [z]
    spot = sum(jnp.where(wanted[i] == diag, i, 0) for i in range(groups))
    late = [jnp.where(i >= spot, wanted[i + 1], wanted[i]) for i in range(groups - 1)] + [diag]

    def unpack(zz, b):
        got = [recvbuf[zz, b, c].astype(F32) for c in range(2)]
        width = nab - main_lanes
        for v in range(vec):
            pieces = []
            for c in range(2):
                body_rows = got[c][v * nij : (v + 1) * nij, :]
                end = got[c][rows : rows + nij, v * width : (v + 1) * width]
                pieces.append(jnp.concatenate([body_rows, end], axis=1))
            out[zz * blocks_here + b, v] = jnp.concatenate(pieces, axis=0).astype(BF16)

    prepare(0, ints, vpairs)
    second("O", 0)
    first("N", 0)
    second("O", 1)
    arrived(other_pairs, pair_recv.at[0])
    arrived(other_ints, pair_recv.at[1])
    prepare(1, other_ints, other_pairs)

    @pl.when(inner)
    def _():
        first("E", 0)
        first("G", 0)
        second("N", 0)
        first("N", 1)
        second("E", 0)
        first("E", 1)
        second("G", 0)
        met(len(peers) - 1)
        first("G", 1)
        cross("G", 1)

    @pl.when(jnp.logical_not(inner))
    def _():

        @pl.when(core == 0)
        def _():
            first("N", 1)
            second("N", 0)
            first("E", 0)
            second("N", 1)
            first("G", 0)
            first("E", 1)
            second("E", 0)
            second("G", 0)
            met(len(peers) - 1)
            first("G", 1)
            cross("G", 1)

        @pl.when(jnp.logical_not(core == 0))
        def _():
            first("N", 1)
            second("N", 0)
            second("N", 1)
            first("E", 0)
            first("G", 0)
            second("E", 0)
            first("E", 1)
            second("G", 0)
            met(len(peers) - 1)
            first("G", 1)
            cross("G", 1)


    pltpu.make_async_copy(gath.at[:, z, chip, 0:bulk], gath.at[:, z, chip, 0:bulk], load_own.at[0]).wait()
    for s in range(groups - 1):
        met(4 + 2 * s)

    @pl.when(inner)
    def _():
        second("N", 1)

    job(0, late[0], late[1])
    second("E", 1)
    job(0, late[2])
    third(0)
    job(0, late[3])
    settled("G", 1)
    job(1, late[0], late[1], late[2])
    third(1)
    job(1, late[3])

    for b in range(blocks_here):
        arrived(recvbuf.at[z, b, 1 - core], o_recv.at[z, b])
        unpack(z, b)
        for s in range(groups - 1):
            zz = far(s)
            arrived(recvbuf.at[zz, b], o_recv.at[zz, b])
            unpack(zz, b)
    left(gath.at[:, 0 : groups - 1, 0], z_send.at[0])
    left(gath.at[0], d_send.at[0])
    left(gath.at[:, :, 0], f_send.at[0])
    left(sendbuf.at[:, 0 : groups - 1], o_send.at[0])
    left(sendbuf.at[:, 0, 0], o_send.at[1])
    left(other_pairs, pair_send.at[0])
    left(other_ints, pair_send.at[1])


def fused(groups, integrals, amplitudes, occupied_energy, virtual_energy, virtual_pairs, occupied_pairs):
    nblk, nef, vec, nij = amplitudes.shape
    here, nab, _ = integrals.shape
    rows = vec * nij
    chips = lax.axis_size("dev") // 2
    amps = jnp.transpose(amplitudes, (0, 2, 3, 1)).reshape(nblk, rows, nef)
    vpairs = jnp.transpose(virtual_pairs, (0, 2, 1))
    opairs = jnp.transpose(occupied_pairs, (1, 0))
    dims = (groups, here, vec, nij, nab, nef)
    dma = pltpu.SemaphoreType.DMA
    arrays = (integrals, amps, occupied_energy, virtual_energy, vpairs, opairs)
    result = pl.pallas_call(
        functools.partial(body, dims),
        out_shape=jax.ShapeDtypeStruct((nblk, vec, 2 * nij, nab), BF16),
        in_specs=[pl.BlockSpec(memory_space=pltpu.HBM)] * 6,
        out_specs=pl.BlockSpec(memory_space=pltpu.VMEM),
        scratch_shapes=[
            pltpu.VMEM(integrals.shape, BF16),
            pltpu.VMEM(amps.shape, BF16),
            pltpu.VMEM(occupied_energy.shape, F32),
            pltpu.VMEM(virtual_energy.shape, F32),
            pltpu.VMEM(vpairs.shape, jnp.int32),
            pltpu.VMEM(opairs.shape, jnp.int32),
            pltpu.VMEM((nblk, rows // 2, LANES), BF16),
            pltpu.VMEM((here, groups, chips, 2 * rows + rows // 2, LANES), BF16),
            pltpu.VMEM(integrals.shape, BF16),
            pltpu.VMEM(vpairs.shape, jnp.int32),
            pltpu.VMEM((here, 2, nab, groups * 3 * LANES), BF16),
            pltpu.VMEM((here, 2, chips, nij, nab), F32),
            pltpu.VMEM((2 * chips * nij, LANES), F32),
            pltpu.VMEM((here, groups, 2, rows + nij, LANES), BF16),
            pltpu.VMEM((groups, here, 2, rows + nij, LANES), BF16),
            pltpu.SemaphoreType.REGULAR((4 + 2 * (groups - 1),)),
            dma((1,)),
            dma((here, groups)),
            dma((1,)),
            dma((here, groups)),
            dma((1,)),
            dma((here,)),
            dma((2,)),
            dma((groups, here)),
            dma((2,)),
            dma((2,)),
            dma((2,)),
            dma((1,)),
            dma((5,)),
        ],
        compiler_params=pltpu.CompilerParams(
            collective_id=0, has_side_effects=True, vmem_limit_bytes=32 * 1024 * 1024
        ),
        name="ladder",
    )(*[pltpu.with_memory_space_constraint(array, pltpu.HBM) for array in arrays])
    return jnp.transpose(result, (0, 3, 1, 2))


def solution(mesh):
    placed = (
        P("grp", "dev", None),
        P(None, "grp", None, "dev"),
        P(),
        P(),
        P("grp", "dev", None),
        P(),
    )
    groups, devs = mesh.shape["grp"], mesh.shape["dev"]

    def local(integrals, amplitudes, *rest):
        nef, vec, nij = amplitudes.shape[1:]
        nab = integrals.shape[1]
        square = devs == 2 * 2 * 2 and devs == 2 * groups
        packs = (
            2 * LANES < nef < 3 * LANES
            and 2 * (nef % LANES) == LANES
            and LANES < nab < 2 * LANES
            and vec * (nab % LANES) == LANES
            and nij % 8 == 0
            and (vec * nij) % 32 == 0
        )
        if square and packs:
            return fused(groups, integrals, amplitudes, *rest)
        return plain(integrals, amplitudes, *rest)

    return jax.shard_map(
        local, mesh=mesh, in_specs=placed, out_specs=P(None, "dev", None, "grp"), check_vma=False
    )
```

```python
import functools

import jax
import jax.numpy as jnp
from jax import lax
from jax.experimental import pallas as pl
from jax.experimental.pallas import tpu as pltpu
from jax.sharding import PartitionSpec as P

LANES = 128
F32 = jnp.float32
BF16 = jnp.bfloat16


def lookup(energy, indices):
    labels = jnp.arange(energy.shape[0], dtype=jnp.int32)
    picked = indices[:, None] == labels[None, :]
    return jnp.sum(jnp.where(picked, energy[None, :], 0.0), axis=1)


def plain(integrals, amplitudes, occupied_energy, virtual_energy, virtual_pairs, occupied_pairs):
    arrived = lax.all_to_all(amplitudes, "grp", split_axis=0, concat_axis=1, tiled=True)
    occ_sum = lookup(occupied_energy, occupied_pairs[:, 0]) + lookup(
        occupied_energy, occupied_pairs[:, 1]
    )
    results = []
    for block in range(arrived.shape[0]):
        panel = arrived[block]
        block_ints = integrals[block]
        gathered = lax.all_gather(panel, "dev", axis=2, tiled=True)
        ladder = jnp.einsum("ae,evj->avj", block_ints, gathered, preferred_element_type=jnp.float32)
        pairs_here = virtual_pairs[block]
        virt_sum = lookup(virtual_energy, pairs_here[:, 0]) + lookup(
            virtual_energy, pairs_here[:, 1]
        )
        denominator = occ_sum[None, :] - virt_sum[:, None]
        results.append((ladder / denominator[:, None, :]).astype(jnp.bfloat16))
    stacked = jnp.stack(results)
    return lax.all_to_all(stacked, "grp", split_axis=3, concat_axis=0, tiled=True)


def as_column(row):
    n = row.shape[1]
    eye = lax.broadcasted_iota(jnp.int32, (n, n), 0) == lax.broadcasted_iota(jnp.int32, (n, n), 1)
    return jnp.sum(jnp.where(eye, jnp.broadcast_to(row, (n, n)), 0.0), axis=1, keepdims=True)


def picked_row(column, index_row):
    shape = (column.shape[0], index_row.shape[1])
    hit = lax.broadcasted_iota(jnp.int32, shape, 0) == jnp.broadcast_to(index_row, shape)
    return jnp.sum(jnp.where(hit, jnp.broadcast_to(column, shape), 0.0), axis=0, keepdims=True)


def body(
    dims,
    ints_hbm,
    amps_hbm,
    occ_e_hbm,
    virt_e_hbm,
    vpairs_hbm,
    opairs_hbm,
    out,
    ints,
    amps,
    occ_e,
    virt_e,
    vpairs,
    opairs,
    tails,
    gath,
    other_ints,
    other_pairs,
    weights,
    recip,
    occ_col,
    sendbuf,
    recvbuf,
    ready,
    z_send,
    z_recv,
    d_send,
    d_recv,
    f_send,
    f_recv,
    o_send,
    o_recv,
    pair_send,
    pair_recv,
    load_amps,
    load_own,
    load_rest,
):
    groups, blocks_here, vec, nij, nab, nef = dims
    rows = vec * nij
    half = rows // 2
    tail = nef % LANES
    main = nef - tail
    bulk = main // LANES * rows
    chunk = bulk + half
    cut = chunk // 32 * 16
    z = lax.axis_index("grp")
    dev = lax.axis_index("dev")
    core = dev % 2
    chip = dev // 2
    flip_x = chip + 1 - 2 * (chip % 2)
    flip_y = chip + 2 - 4 * (chip // 2)
    diag = 3 - chip
    mesh_id = pl.DeviceIdType.MESH

    def at(zz, pp, cc):
        return (zz, pp * 2 + cc)

    low = z < groups // 2

    def far(step):
        down = groups - 1 - step
        down = down - jnp.where(down <= z, 1, 0)
        up = step + jnp.where(step >= z, 1, 0)
        return jnp.where(low, down, up)

    def across(step):
        return jnp.where(low, groups // 2 + step, groups // 2 - 1 - step)

    def reach(step):
        return jnp.where(step < z, z - 1 - step, step + 1)

    loads = []
    for b in range(blocks_here):
        loads.append(pltpu.make_async_copy(amps_hbm.at[z * blocks_here + b], amps.at[b], load_amps.at[0]))
    for s in range(groups - 1):
        for b in range(blocks_here):
            slot = (s + 1) * blocks_here + b
            loads.append(
                pltpu.make_async_copy(amps_hbm.at[reach(s) * blocks_here + b], amps.at[slot], load_amps.at[1])
            )

    def bulk_parts(block, piece):
        for i in range(main // LANES):
            yield amps_hbm.at[block, :, i * LANES : (i + 1) * LANES], piece.at[i * rows : (i + 1) * rows]

    for b in range(blocks_here):
        for src, dst in bulk_parts(z * blocks_here + b, gath.at[b, z, chip]):
            loads.append(pltpu.make_async_copy(src, dst, load_own.at[0]))
    pairs = [(ints_hbm, ints), (occ_e_hbm, occ_e), (virt_e_hbm, virt_e), (vpairs_hbm, vpairs), (opairs_hbm, opairs)]
    rest = [pltpu.make_async_copy(src, dst, load_rest.at[i]) for i, (src, dst) in enumerate(pairs)]

    partner = at(z, chip, 1 - core)
    x_peer = at(z, flip_x, core)
    y_peer = at(z, flip_y, core)
    swap = chip == 2
    ways = [
        at(z, jnp.where(swap, flip_y, flip_x), core),
        at(z, jnp.where(swap, flip_x, flip_y), core),
    ]
    peers = [(partner, core == 0, 0), (x_peer, chip % 2 == 0, 1), (y_peer, chip < 2, 2)]
    last = 3 + 2 * (groups - 1)
    for s in range(groups - 1):
        zz = reach(s)
        for c in range(2):
            peers.append((at(zz, chip, core if c == 0 else 1 - core), zz > z, 3 + s * 2 + c))
    d_peer = at(z, diag, core)
    peers.append((d_peer, chip < 2, last))
    barrier = pltpu.get_barrier_semaphore()
    for peer, higher, _ in peers:
        @pl.when(higher)
        def _(peer=peer):
            pl.semaphore_signal(barrier, inc=1, device_id=peer, device_id_type=mesh_id)
    for load in loads + rest:
        load.start()
    earlier = 2 * z + chip + core

    @pl.when(earlier > 0)
    def _():
        pl.semaphore_wait(barrier, earlier)

    for i, (peer, higher, slot) in enumerate(peers):
        if i < 3 or slot == last:
            there = slot
        else:
            s, c = (i - 3) // 2, (i - 3) % 2
            zz = reach(s)
            there = 3 + c + 2 * jnp.where(z < zz, zz - 1 - z, z - 1)

        @pl.when(jnp.logical_not(higher))
        def _(peer=peer, there=there):
            pl.semaphore_signal(ready.at[there], inc=1, device_id=peer, device_id_type=mesh_id)

    def met_z(name):
        spot = outlets[name][1]
        higher = outlets[name][0] > z

        @pl.when(higher)
        def _():
            pl.semaphore_wait(ready.at[3 + 2 * spot], 1)

    def met(i):
        @pl.when(peers[i][1])
        def _():
            pl.semaphore_wait(ready.at[peers[i][2]], 1)

    def met_way(way):
        i = jnp.where(swap, 2 - way, 1 + way)
        higher = jnp.where(i == 1, chip % 2 == 0, chip < 2)

        @pl.when(higher)
        def _():
            pl.semaphore_wait(ready.at[i], 1)

    def send(src, dst, ssem, rsem, to):
        pltpu.make_async_remote_copy(
            src_ref=src, dst_ref=dst, send_sem=ssem, recv_sem=rsem, device_id=to, device_id_type=mesh_id
        ).start()

    def whole(ref, sem):
        return pltpu.make_async_remote_copy(
            src_ref=ref, dst_ref=ref, send_sem=sem, recv_sem=sem, device_id=partner, device_id_type=mesh_id
        )

    def arrived(ref, sem):
        whole(ref, sem).wait_recv()

    def left(ref, sem):
        whole(ref, sem).wait_send()

    near = z + 1 - 2 * (z % 2)
    inner = jnp.logical_and(z > 0, z < groups - 1)
    sources = {"O": (z, z), "N": (near, near), "C": (across(0),) * 2, "D": (across(1),) * 2}
    turn = [
        jnp.where(jnp.logical_or(z == groups - 1, jnp.logical_and(core == 0, z != 1)), 1, 0),
        jnp.where(jnp.logical_and(core == 1, z == 1), 0, 1),
    ]
    sources["E"] = tuple(across(t) for t in turn)
    sources["G"] = tuple(across(1 - t) for t in turn)

    def direct_main(b, way):
        for src, dst in bulk_parts(z * blocks_here + b, gath.at[b, z, chip]):
            send(src, dst, d_send.at[0], d_recv.at[b, z], ways[way])

    def direct_tail(b, way):
        send(tails.at[b], gath.at[b, z, chip, bulk:chunk], d_send.at[0], d_recv.at[b, z], ways[way])

    skip = jnp.where(z == 2, 0, 1)
    outlets = {"N": (near, 2 * (1 - skip)), "C": (across(0), skip), "D": (across(1), skip + 1)}

    def inward_main(name, b):
        to = outlets[name][0]
        for src, dst in bulk_parts(to * blocks_here + b, gath.at[b, z, chip]):
            send(src, dst, z_send.at[0], z_recv.at[b, z], at(to, chip, core))

    def inward_tail(name, b):
        to, spot = outlets[name]
        send(
            tails.at[(spot + 1) * blocks_here + b], gath.at[b, z, chip, bulk:chunk],
            z_send.at[0], z_recv.at[b, z], at(to, chip, core),
        )

    def first(name, b):
        zz = sources[name][b]
        piece = gath.at[b, zz, chip]
        arrived(piece, z_recv.at[b, zz])
        for peer in (x_peer, y_peer):
            send(piece, piece, d_send.at[0], d_recv.at[b, zz], peer)

    def second(name, b):
        zz = sources[name][b]
        arrived(gath.at[b, zz, 0:2], d_recv.at[b, zz])
        src = gath.at[b, zz, flip_x, 0:cut]
        send(src, src, f_send.at[0], f_recv.at[b], y_peer)
        src = gath.at[b, zz, flip_y, cut:chunk]
        send(src, src, f_send.at[0], f_recv.at[b], x_peer)

    def cross(name, b):
        piece = gath.at[b, sources[name][b], chip]
        send(piece, piece, f_send.at[0], f_recv.at[b], d_peer)

    def settled(name, b):
        arrived(gath.at[b, sources[name][b], 0:2], d_recv.at[b, sources[name][b]])

    def third(b):
        arrived(gath.at[b, :, diag], f_recv.at[b])

    def pack(slot):
        lower = amps[slot, 0:half, main:nef].astype(F32)
        upper = amps[slot, half:rows, main:nef].astype(F32)
        tails[slot] = jnp.concatenate([lower, upper], axis=1).astype(BF16)

    def loaded(slots, sem):
        pltpu.make_async_copy(amps.at[slots], amps.at[slots], sem).wait()


    @pl.when(chip == 3)
    def _():
        met_way(0)
        direct_main(0, 0)
        met_way(1)
        direct_main(0, 1)

        @pl.when(jnp.logical_not(inner))
        def _():
            met_z("N")
            inward_main("N", 0)

        loaded(slice(0, blocks_here), load_amps.at[0])
        for b in range(blocks_here):
            pack(b)
        direct_tail(0, 0)
        direct_tail(0, 1)
        direct_main(1, 0)
        direct_main(1, 1)
        direct_tail(1, 0)
        direct_tail(1, 1)
        loaded(slice(blocks_here, groups * blocks_here), load_amps.at[1])
        for slot in range(blocks_here, groups * blocks_here):
            pack(slot)

    @pl.when(jnp.logical_not(chip == 3))
    def _():

        @pl.when(jnp.logical_not(chip == 0))
        def _():
            met_way(0)
            direct_main(0, 0)


        @pl.when(jnp.logical_not(inner))
        def _():
            met_z("N")
            inward_main("N", 0)

        loaded(slice(0, blocks_here), load_amps.at[0])
        for b in range(blocks_here):
            pack(b)
        loaded(slice(blocks_here, groups * blocks_here), load_amps.at[1])
        for slot in range(blocks_here, groups * blocks_here):
            pack(slot)

        @pl.when(chip == 0)
        def _():
            met_way(0)
            direct_main(0, 0)


        @pl.when(jnp.logical_not(inner))
        def _():
            inward_tail("N", 0)

        direct_tail(0, 0)
        direct_main(1, 0)
        direct_tail(1, 0)

        @pl.when(inner)
        def _():

            @pl.when(z == 2)
            def _():

                @pl.when(core == 0)
                def _():
                    met_z("C")
                    inward_main("C", 0)
                    inward_tail("C", 0)
                    met_z("D")
                    inward_main("D", 0)
                    inward_tail("D", 0)
                    met_z("N")
                    inward_main("N", 0)
                    inward_tail("N", 0)
                    inward_main("C", 1)
                    inward_tail("C", 1)
                    inward_main("D", 1)
                    inward_tail("D", 1)
                    inward_main("N", 1)
                    inward_tail("N", 1)

                @pl.when(jnp.logical_not(core == 0))
                def _():
                    met_z("C")
                    inward_main("C", 0)
                    inward_tail("C", 0)
                    met_z("D")
                    inward_main("D", 0)
                    inward_tail("D", 0)
                    met_z("N")
                    inward_main("N", 0)
                    inward_tail("N", 0)
                    inward_main("C", 1)
                    inward_tail("C", 1)
                    inward_main("D", 1)
                    inward_tail("D", 1)
                    inward_main("N", 1)
                    inward_tail("N", 1)


            @pl.when(jnp.logical_not(z == 2))
            def _():

                @pl.when(core == 0)
                def _():
                    met_z("N")
                    inward_main("N", 0)
                    inward_tail("N", 0)
                    met_z("C")
                    inward_main("C", 0)
                    inward_tail("C", 0)
                    met_z("D")
                    inward_main("D", 0)
                    inward_tail("D", 0)
                    inward_main("N", 1)
                    inward_tail("N", 1)
                    inward_main("C", 1)
                    inward_tail("C", 1)
                    inward_main("D", 1)
                    inward_tail("D", 1)

                @pl.when(jnp.logical_not(core == 0))
                def _():
                    met_z("N")
                    inward_main("N", 0)
                    inward_tail("N", 0)
                    met_z("C")
                    inward_main("C", 0)
                    inward_tail("C", 0)
                    met_z("D")
                    inward_main("D", 0)
                    inward_tail("D", 0)
                    inward_main("N", 1)
                    inward_tail("N", 1)
                    inward_main("C", 1)
                    inward_tail("C", 1)
                    inward_main("D", 1)
                    inward_tail("D", 1)


        @pl.when(jnp.logical_not(inner))
        def _():
            met_z("C")
            inward_main("C", 0)
            inward_tail("C", 0)

        met_way(1)
        direct_main(0, 1)
        direct_tail(0, 1)
        direct_main(1, 1)
        direct_tail(1, 1)


    @pl.when(chip == 3)
    def _():

        @pl.when(inner)
        def _():

            @pl.when(z == 2)
            def _():

                @pl.when(core == 0)
                def _():
                    met_z("C")
                    inward_main("C", 0)
                    inward_tail("C", 0)
                    met_z("D")
                    inward_main("D", 0)
                    inward_tail("D", 0)
                    met_z("N")
                    inward_main("N", 0)
                    inward_tail("N", 0)
                    inward_main("C", 1)
                    inward_tail("C", 1)
                    inward_main("D", 1)
                    inward_tail("D", 1)
                    inward_main("N", 1)
                    inward_tail("N", 1)

                @pl.when(jnp.logical_not(core == 0))
                def _():
                    met_z("C")
                    inward_main("C", 0)
                    inward_tail("C", 0)
                    met_z("D")
                    inward_main("D", 0)
                    inward_tail("D", 0)
                    met_z("N")
                    inward_main("N", 0)
                    inward_tail("N", 0)
                    inward_main("C", 1)
                    inward_tail("C", 1)
                    inward_main("D", 1)
                    inward_tail("D", 1)
                    inward_main("N", 1)
                    inward_tail("N", 1)


            @pl.when(jnp.logical_not(z == 2))
            def _():

                @pl.when(core == 0)
                def _():
                    met_z("N")
                    inward_main("N", 0)
                    inward_tail("N", 0)
                    met_z("C")
                    inward_main("C", 0)
                    inward_tail("C", 0)
                    met_z("D")
                    inward_main("D", 0)
                    inward_tail("D", 0)
                    inward_main("N", 1)
                    inward_tail("N", 1)
                    inward_main("C", 1)
                    inward_tail("C", 1)
                    inward_main("D", 1)
                    inward_tail("D", 1)

                @pl.when(jnp.logical_not(core == 0))
                def _():
                    met_z("N")
                    inward_main("N", 0)
                    inward_tail("N", 0)
                    met_z("C")
                    inward_main("C", 0)
                    inward_tail("C", 0)
                    met_z("D")
                    inward_main("D", 0)
                    inward_tail("D", 0)
                    inward_main("N", 1)
                    inward_tail("N", 1)
                    inward_main("C", 1)
                    inward_tail("C", 1)
                    inward_main("D", 1)
                    inward_tail("D", 1)


        @pl.when(jnp.logical_not(inner))
        def _():
            inward_tail("N", 0)
            met_z("C")
            inward_main("C", 0)
            inward_tail("C", 0)
            met_z("D")
            inward_main("D", 0)
            inward_tail("D", 0)
            inward_main("N", 1)
            inward_tail("N", 1)
            inward_main("C", 1)
            inward_tail("C", 1)
            inward_main("D", 1)
            inward_tail("D", 1)


    @pl.when(jnp.logical_not(chip == 3))
    def _():

        @pl.when(jnp.logical_not(inner))
        def _():
            met_z("D")
            inward_main("D", 0)
            inward_tail("D", 0)
            inward_main("N", 1)
            inward_tail("N", 1)
            inward_main("C", 1)
            inward_tail("C", 1)
            inward_main("D", 1)
            inward_tail("D", 1)


    met(0)
    send(vpairs_hbm, other_pairs, pair_send.at[0], pair_recv.at[0], partner)
    send(ints_hbm, other_ints, pair_send.at[1], pair_recv.at[1], partner)
    for b in range(blocks_here):
        gath[b, z, chip, bulk:chunk] = tails[b]
    for load in rest:
        load.wait()

    occ_column = as_column(occ_e[...].reshape(1, -1))
    occ_row = picked_row(occ_column, opairs[0:1, :]) + picked_row(occ_column, opairs[1:2, :])
    occ_col[...] = jnp.broadcast_to(as_column(occ_row), occ_col.shape)
    virt_column = as_column(virt_e[...].reshape(1, -1))

    def prepare(side, int_ref, pair_ref):
        for b in range(blocks_here):
            virt_row = picked_row(virt_column, pair_ref[b, 0:1, :]) + picked_row(
                virt_column, pair_ref[b, 1:2, :]
            )
            for p in range(gath.shape[2]):
                start = pl.multiple_of((2 * p + core) * nij, 8)
                occ = occ_col[pl.ds(start, nij), 0:1]
                recip[b, side, p] = 1.0 / (occ - virt_row)
            for zz in range(groups):
                panel = int_ref[b, :, zz * nef : (zz + 1) * nef].astype(F32)
                last = panel[:, main:nef]
                wide = jnp.concatenate([panel[:, 0:main], last, last], axis=1)
                width = main + LANES
                weights[b, side, :, zz * width : (zz + 1) * width] = wide.astype(BF16)

    lane = lax.broadcasted_iota(jnp.int32, (half, LANES), 1)
    main_lanes = nab // LANES * LANES

    def job(b, *columns):
        panels = []
        for p in columns:
            parts = []
            for zz in range(groups):
                end = gath[b, zz, p, bulk:chunk]
                zero = jnp.zeros_like(end)
                end2 = jnp.concatenate(
                    [jnp.where(lane < tail, end, zero), jnp.where(lane < tail, zero, end)], axis=0
                )
                parts += [gath[b, zz, p, i * rows : (i + 1) * rows] for i in range(main // LANES)] + [end2]
            panels.append(jnp.concatenate(parts, axis=1))
        panel = jnp.concatenate(panels, axis=0)
        for side in range(2):
            total = lax.dot_general(
                panel, weights[b, side], (((1,), (1,)), ((), ())), preferred_element_type=F32
            )
            for i, p in enumerate(columns):
                scaled = total[i * rows : (i + 1) * rows].reshape(vec, nij, nab) * recip[b, side, p][None]
                ends = [scaled[v, :, main_lanes:nab] for v in range(vec)]
                sendbuf[b, p, side, 0:rows, :] = scaled[:, :, 0:main_lanes].reshape(rows, main_lanes).astype(BF16)
                sendbuf[b, p, side, rows : rows + nij, :] = jnp.concatenate(ends, axis=1).astype(BF16)
        for p in columns:
            deliver(b, p)

    def deliver(b, p):
        @pl.when(p != z)
        def _():
            for side in range(2):
                send(
                    sendbuf.at[b, p, side], recvbuf.at[z, b, core], o_send.at[0], o_recv.at[z, b],
                    at(p, chip, core if side == 0 else 1 - core),
                )

        @pl.when(p == z)
        def _():
            send(sendbuf.at[b, z, 1], recvbuf.at[z, b, core], o_send.at[1], o_recv.at[z, b], partner)
            recvbuf[z, b, core] = sendbuf[b, z, 0]

    wanted = [far(s) for s in range(groups - 1)] + [z]
    spot = sum(jnp.where(wanted[i] == diag, i, 0) for i in range(groups))
    late = [jnp.where(i >= spot, wanted[i + 1], wanted[i]) for i in range(groups - 1)] + [diag]

    def unpack(zz, b):
        got = [recvbuf[zz, b, c].astype(F32) for c in range(2)]
        width = nab - main_lanes
        for v in range(vec):
            pieces = []
            for c in range(2):
                body_rows = got[c][v * nij : (v + 1) * nij, :]
                end = got[c][rows : rows + nij, v * width : (v + 1) * width]
                pieces.append(jnp.concatenate([body_rows, end], axis=1))
            out[zz * blocks_here + b, v] = jnp.concatenate(pieces, axis=0).astype(BF16)

    second("O", 0)
    prepare(0, ints, vpairs)
    first("N", 0)
    second("O", 1)
    arrived(other_pairs, pair_recv.at[0])
    arrived(other_ints, pair_recv.at[1])
    prepare(1, other_ints, other_pairs)

    @pl.when(inner)
    def _():
        first("E", 0)
        first("G", 0)
        second("N", 0)
        second("E", 0)
        first("N", 1)
        first("E", 1)
        second("G", 0)
        met(len(peers) - 1)
        first("G", 1)
        cross("G", 1)

    @pl.when(jnp.logical_not(inner))
    def _():

        @pl.when(core == 0)
        def _():
            first("N", 1)
            second("N", 0)
            first("E", 0)
            second("N", 1)
            first("G", 0)
            first("E", 1)
            second("E", 0)
            second("G", 0)
            met(len(peers) - 1)
            first("G", 1)
            cross("G", 1)

        @pl.when(jnp.logical_not(core == 0))
        def _():
            first("N", 1)
            second("N", 0)
            second("N", 1)
            first("E", 0)
            first("G", 0)
            second("E", 0)
            first("E", 1)
            second("G", 0)
            met(len(peers) - 1)
            first("G", 1)
            cross("G", 1)


    pltpu.make_async_copy(gath.at[:, z, chip, 0:bulk], gath.at[:, z, chip, 0:bulk], load_own.at[0]).wait()
    for s in range(groups - 1):
        met(4 + 2 * s)
    job(0, late[0], late[1])

    @pl.when(inner)
    def _():
        second("N", 1)

    second("E", 1)
    job(0, late[2])
    third(0)
    job(0, late[3])
    settled("G", 1)
    job(1, late[0], late[1], late[2])
    third(1)
    job(1, late[3])

    for b in range(blocks_here):
        arrived(recvbuf.at[z, b, 1 - core], o_recv.at[z, b])
        unpack(z, b)
        for s in range(groups - 1):
            zz = far(s)
            arrived(recvbuf.at[zz, b], o_recv.at[zz, b])
            unpack(zz, b)
    left(gath.at[:, 0 : groups - 1, 0], z_send.at[0])
    left(gath.at[0], d_send.at[0])
    left(gath.at[:, :, 0], f_send.at[0])
    left(sendbuf.at[:, 0 : groups - 1], o_send.at[0])
    left(sendbuf.at[:, 0, 0], o_send.at[1])
    left(other_pairs, pair_send.at[0])
    left(other_ints, pair_send.at[1])


def fused(groups, integrals, amplitudes, occupied_energy, virtual_energy, virtual_pairs, occupied_pairs):
    nblk, nef, vec, nij = amplitudes.shape
    here, nab, _ = integrals.shape
    rows = vec * nij
    chips = lax.axis_size("dev") // 2
    amps = jnp.transpose(amplitudes, (0, 2, 3, 1)).reshape(nblk, rows, nef)
    vpairs = jnp.transpose(virtual_pairs, (0, 2, 1))
    opairs = jnp.transpose(occupied_pairs, (1, 0))
    dims = (groups, here, vec, nij, nab, nef)
    dma = pltpu.SemaphoreType.DMA
    arrays = (integrals, amps, occupied_energy, virtual_energy, vpairs, opairs)
    result = pl.pallas_call(
        functools.partial(body, dims),
        out_shape=jax.ShapeDtypeStruct((nblk, vec, 2 * nij, nab), BF16),
        in_specs=[pl.BlockSpec(memory_space=pltpu.HBM)] * 6,
        out_specs=pl.BlockSpec(memory_space=pltpu.VMEM),
        scratch_shapes=[
            pltpu.VMEM(integrals.shape, BF16),
            pltpu.VMEM(amps.shape, BF16),
            pltpu.VMEM(occupied_energy.shape, F32),
            pltpu.VMEM(virtual_energy.shape, F32),
            pltpu.VMEM(vpairs.shape, jnp.int32),
            pltpu.VMEM(opairs.shape, jnp.int32),
            pltpu.VMEM((nblk, rows // 2, LANES), BF16),
            pltpu.VMEM((here, groups, chips, 2 * rows + rows // 2, LANES), BF16),
            pltpu.VMEM(integrals.shape, BF16),
            pltpu.VMEM(vpairs.shape, jnp.int32),
            pltpu.VMEM((here, 2, nab, groups * 3 * LANES), BF16),
            pltpu.VMEM((here, 2, chips, nij, nab), F32),
            pltpu.VMEM((2 * chips * nij, LANES), F32),
            pltpu.VMEM((here, groups, 2, rows + nij, LANES), BF16),
            pltpu.VMEM((groups, here, 2, rows + nij, LANES), BF16),
            pltpu.SemaphoreType.REGULAR((4 + 2 * (groups - 1),)),
            dma((1,)),
            dma((here, groups)),
            dma((1,)),
            dma((here, groups)),
            dma((1,)),
            dma((here,)),
            dma((2,)),
            dma((groups, here)),
            dma((2,)),
            dma((2,)),
            dma((2,)),
            dma((1,)),
            dma((5,)),
        ],
        compiler_params=pltpu.CompilerParams(
            collective_id=0, has_side_effects=True, vmem_limit_bytes=32 * 1024 * 1024
        ),
        name="ladder",
    )(*[pltpu.with_memory_space_constraint(array, pltpu.HBM) for array in arrays])
    return jnp.transpose(result, (0, 3, 1, 2))


def solution(mesh):
    placed = (
        P("grp", "dev", None),
        P(None, "grp", None, "dev"),
        P(),
        P(),
        P("grp", "dev", None),
        P(),
    )
    groups, devs = mesh.shape["grp"], mesh.shape["dev"]

    def local(integrals, amplitudes, *rest):
        nef, vec, nij = amplitudes.shape[1:]
        nab = integrals.shape[1]
        square = devs == 2 * 2 * 2 and devs == 2 * groups
        packs = (
            2 * LANES < nef < 3 * LANES
            and 2 * (nef % LANES) == LANES
            and LANES < nab < 2 * LANES
            and vec * (nab % LANES) == LANES
            and nij % 8 == 0
            and (vec * nij) % 32 == 0
        )
        if square and packs:
            return fused(groups, integrals, amplitudes, *rest)
        return plain(integrals, amplitudes, *rest)

    return jax.shard_map(
        local, mesh=mesh, in_specs=placed, out_specs=P(None, "dev", None, "grp"), check_vma=False
    )
```

```python
import functools

import jax
import jax.numpy as jnp
from jax import lax
from jax.experimental import pallas as pl
from jax.experimental.pallas import tpu as pltpu
from jax.sharding import PartitionSpec as P

LANES = 128
F32 = jnp.float32
BF16 = jnp.bfloat16


def lookup(energy, indices):
    labels = jnp.arange(energy.shape[0], dtype=jnp.int32)
    picked = indices[:, None] == labels[None, :]
    return jnp.sum(jnp.where(picked, energy[None, :], 0.0), axis=1)


def plain(integrals, amplitudes, occupied_energy, virtual_energy, virtual_pairs, occupied_pairs):
    arrived = lax.all_to_all(amplitudes, "grp", split_axis=0, concat_axis=1, tiled=True)
    occ_sum = lookup(occupied_energy, occupied_pairs[:, 0]) + lookup(
        occupied_energy, occupied_pairs[:, 1]
    )
    results = []
    for block in range(arrived.shape[0]):
        panel = arrived[block]
        block_ints = integrals[block]
        gathered = lax.all_gather(panel, "dev", axis=2, tiled=True)
        ladder = jnp.einsum("ae,evj->avj", block_ints, gathered, preferred_element_type=jnp.float32)
        pairs_here = virtual_pairs[block]
        virt_sum = lookup(virtual_energy, pairs_here[:, 0]) + lookup(
            virtual_energy, pairs_here[:, 1]
        )
        denominator = occ_sum[None, :] - virt_sum[:, None]
        results.append((ladder / denominator[:, None, :]).astype(jnp.bfloat16))
    stacked = jnp.stack(results)
    return lax.all_to_all(stacked, "grp", split_axis=3, concat_axis=0, tiled=True)


def as_column(row):
    n = row.shape[1]
    eye = lax.broadcasted_iota(jnp.int32, (n, n), 0) == lax.broadcasted_iota(jnp.int32, (n, n), 1)
    return jnp.sum(jnp.where(eye, jnp.broadcast_to(row, (n, n)), 0.0), axis=1, keepdims=True)


def picked_row(column, index_row):
    shape = (column.shape[0], index_row.shape[1])
    hit = lax.broadcasted_iota(jnp.int32, shape, 0) == jnp.broadcast_to(index_row, shape)
    return jnp.sum(jnp.where(hit, jnp.broadcast_to(column, shape), 0.0), axis=0, keepdims=True)


def body(
    dims,
    ints_hbm,
    amps_hbm,
    occ_e_hbm,
    virt_e_hbm,
    vpairs_hbm,
    opairs_hbm,
    out,
    ints,
    amps,
    occ_e,
    virt_e,
    vpairs,
    opairs,
    tails,
    gath,
    other_ints,
    other_pairs,
    weights,
    recip,
    occ_col,
    sendbuf,
    recvbuf,
    ready,
    z_send,
    z_recv,
    d_send,
    d_recv,
    f_send,
    f_recv,
    o_send,
    o_recv,
    pair_send,
    pair_recv,
    load_amps,
    load_own,
    load_rest,
):
    groups, blocks_here, vec, nij, nab, nef = dims
    rows = vec * nij
    half = rows // 2
    tail = nef % LANES
    main = nef - tail
    bulk = main // LANES * rows
    chunk = bulk + half
    cut = chunk // 32 * 16
    z = lax.axis_index("grp")
    dev = lax.axis_index("dev")
    core = dev % 2
    chip = dev // 2
    flip_x = chip + 1 - 2 * (chip % 2)
    flip_y = chip + 2 - 4 * (chip // 2)
    diag = 3 - chip
    mesh_id = pl.DeviceIdType.MESH

    def at(zz, pp, cc):
        return (zz, pp * 2 + cc)

    low = z < groups // 2

    def far(step):
        down = groups - 1 - step
        down = down - jnp.where(down <= z, 1, 0)
        up = step + jnp.where(step >= z, 1, 0)
        return jnp.where(low, down, up)

    def across(step):
        return jnp.where(low, groups // 2 + step, groups // 2 - 1 - step)

    def reach(step):
        return jnp.where(step < z, z - 1 - step, step + 1)

    loads = []
    for b in range(blocks_here):
        loads.append(pltpu.make_async_copy(amps_hbm.at[z * blocks_here + b], amps.at[b], load_amps.at[0]))
    for s in range(groups - 1):
        for b in range(blocks_here):
            slot = (s + 1) * blocks_here + b
            loads.append(
                pltpu.make_async_copy(amps_hbm.at[reach(s) * blocks_here + b], amps.at[slot], load_amps.at[1])
            )

    def bulk_parts(block, piece):
        for i in range(main // LANES):
            yield amps_hbm.at[block, :, i * LANES : (i + 1) * LANES], piece.at[i * rows : (i + 1) * rows]

    for b in range(blocks_here):
        for src, dst in bulk_parts(z * blocks_here + b, gath.at[b, z, chip]):
            loads.append(pltpu.make_async_copy(src, dst, load_own.at[0]))
    pairs = [(ints_hbm, ints), (occ_e_hbm, occ_e), (virt_e_hbm, virt_e), (vpairs_hbm, vpairs), (opairs_hbm, opairs)]
    rest = [pltpu.make_async_copy(src, dst, load_rest.at[i]) for i, (src, dst) in enumerate(pairs)]

    partner = at(z, chip, 1 - core)
    x_peer = at(z, flip_x, core)
    y_peer = at(z, flip_y, core)
    swap = chip == 2
    ways = [
        at(z, jnp.where(swap, flip_y, flip_x), core),
        at(z, jnp.where(swap, flip_x, flip_y), core),
    ]
    peers = [(partner, core == 0, 0), (x_peer, chip % 2 == 0, 1), (y_peer, chip < 2, 2)]
    last = 3 + 2 * (groups - 1)
    for s in range(groups - 1):
        zz = reach(s)
        for c in range(2):
            peers.append((at(zz, chip, core if c == 0 else 1 - core), zz > z, 3 + s * 2 + c))
    d_peer = at(z, diag, core)
    peers.append((d_peer, chip < 2, last))
    barrier = pltpu.get_barrier_semaphore()
    for peer, higher, _ in peers:
        @pl.when(higher)
        def _(peer=peer):
            pl.semaphore_signal(barrier, inc=1, device_id=peer, device_id_type=mesh_id)
    for load in loads + rest:
        load.start()
    earlier = 2 * z + chip + core

    @pl.when(earlier > 0)
    def _():
        pl.semaphore_wait(barrier, earlier)

    for i, (peer, higher, slot) in enumerate(peers):
        if i < 3 or slot == last:
            there = slot
        else:
            s, c = (i - 3) // 2, (i - 3) % 2
            zz = reach(s)
            there = 3 + c + 2 * jnp.where(z < zz, zz - 1 - z, z - 1)

        @pl.when(jnp.logical_not(higher))
        def _(peer=peer, there=there):
            pl.semaphore_signal(ready.at[there], inc=1, device_id=peer, device_id_type=mesh_id)

    def met_z(name):
        spot = outlets[name][1]
        higher = outlets[name][0] > z

        @pl.when(higher)
        def _():
            pl.semaphore_wait(ready.at[3 + 2 * spot], 1)

    def met(i):
        @pl.when(peers[i][1])
        def _():
            pl.semaphore_wait(ready.at[peers[i][2]], 1)

    def met_way(way):
        i = jnp.where(swap, 2 - way, 1 + way)
        higher = jnp.where(i == 1, chip % 2 == 0, chip < 2)

        @pl.when(higher)
        def _():
            pl.semaphore_wait(ready.at[i], 1)

    def send(src, dst, ssem, rsem, to):
        pltpu.make_async_remote_copy(
            src_ref=src, dst_ref=dst, send_sem=ssem, recv_sem=rsem, device_id=to, device_id_type=mesh_id
        ).start()

    def whole(ref, sem):
        return pltpu.make_async_remote_copy(
            src_ref=ref, dst_ref=ref, send_sem=sem, recv_sem=sem, device_id=partner, device_id_type=mesh_id
        )

    def arrived(ref, sem):
        whole(ref, sem).wait_recv()

    def left(ref, sem):
        whole(ref, sem).wait_send()

    near = z + 1 - 2 * (z % 2)
    inner = jnp.logical_and(z > 0, z < groups - 1)
    sources = {"O": (z, z), "N": (near, near), "C": (across(0),) * 2, "D": (across(1),) * 2}
    turn = [
        jnp.where(jnp.logical_or(z == groups - 1, jnp.logical_and(core == 0, z != 1)), 1, 0),
        jnp.where(jnp.logical_and(core == 1, z == 1), 0, 1),
    ]
    sources["E"] = tuple(across(t) for t in turn)
    sources["G"] = tuple(across(1 - t) for t in turn)

    def direct_main(b, way):
        for src, dst in bulk_parts(z * blocks_here + b, gath.at[b, z, chip]):
            send(src, dst, d_send.at[0], d_recv.at[b, z], ways[way])

    def direct_tail(b, way):
        send(tails.at[b], gath.at[b, z, chip, bulk:chunk], d_send.at[0], d_recv.at[b, z], ways[way])

    skip = jnp.where(z == 2, 0, 1)
    outlets = {"N": (near, 2 * (1 - skip)), "C": (across(0), skip), "D": (across(1), skip + 1)}

    def inward_main(name, b):
        to = outlets[name][0]
        for src, dst in bulk_parts(to * blocks_here + b, gath.at[b, z, chip]):
            send(src, dst, z_send.at[0], z_recv.at[b, z], at(to, chip, core))

    def inward_tail(name, b):
        to, spot = outlets[name]
        send(
            tails.at[(spot + 1) * blocks_here + b], gath.at[b, z, chip, bulk:chunk],
            z_send.at[0], z_recv.at[b, z], at(to, chip, core),
        )

    def first(name, b):
        zz = sources[name][b]
        piece = gath.at[b, zz, chip]
        arrived(piece, z_recv.at[b, zz])
        for peer in (x_peer, y_peer):
            send(piece, piece, d_send.at[0], d_recv.at[b, zz], peer)

    def second(name, b):
        zz = sources[name][b]
        arrived(gath.at[b, zz, 0:2], d_recv.at[b, zz])
        src = gath.at[b, zz, flip_x, 0:cut]
        send(src, src, f_send.at[0], f_recv.at[b], y_peer)
        src = gath.at[b, zz, flip_y, cut:chunk]
        send(src, src, f_send.at[0], f_recv.at[b], x_peer)

    def cross(name, b):
        piece = gath.at[b, sources[name][b], chip]
        send(piece, piece, f_send.at[0], f_recv.at[b], d_peer)

    def settled(name, b):
        arrived(gath.at[b, sources[name][b], 0:2], d_recv.at[b, sources[name][b]])

    def third(b):
        arrived(gath.at[b, :, diag], f_recv.at[b])

    def pack(slot):
        lower = amps[slot, 0:half, main:nef].astype(F32)
        upper = amps[slot, half:rows, main:nef].astype(F32)
        tails[slot] = jnp.concatenate([lower, upper], axis=1).astype(BF16)

    def loaded(slots, sem):
        pltpu.make_async_copy(amps.at[slots], amps.at[slots], sem).wait()


    @pl.when(chip == 3)
    def _():
        met_way(0)
        direct_main(0, 0)
        met_way(1)
        direct_main(0, 1)

        @pl.when(jnp.logical_not(inner))
        def _():
            met_z("N")
            inward_main("N", 0)

        loaded(slice(0, blocks_here), load_amps.at[0])
        for b in range(blocks_here):
            pack(b)
        direct_tail(0, 0)
        direct_tail(0, 1)
        direct_main(1, 0)
        direct_main(1, 1)
        direct_tail(1, 0)
        direct_tail(1, 1)
        loaded(slice(blocks_here, groups * blocks_here), load_amps.at[1])
        for slot in range(blocks_here, groups * blocks_here):
            pack(slot)

    @pl.when(jnp.logical_not(chip == 3))
    def _():

        @pl.when(jnp.logical_not(chip == 0))
        def _():
            met_way(0)
            direct_main(0, 0)


        @pl.when(jnp.logical_not(inner))
        def _():
            met_z("N")
            inward_main("N", 0)

        loaded(slice(0, blocks_here), load_amps.at[0])
        for b in range(blocks_here):
            pack(b)
        loaded(slice(blocks_here, groups * blocks_here), load_amps.at[1])
        for slot in range(blocks_here, groups * blocks_here):
            pack(slot)

        @pl.when(chip == 0)
        def _():
            met_way(0)
            direct_main(0, 0)


        @pl.when(jnp.logical_not(inner))
        def _():
            inward_tail("N", 0)

        direct_tail(0, 0)
        direct_main(1, 0)
        direct_tail(1, 0)

        @pl.when(inner)
        def _():

            @pl.when(z == 2)
            def _():

                @pl.when(core == 0)
                def _():
                    met_z("C")
                    inward_main("C", 0)
                    inward_tail("C", 0)
                    met_z("D")
                    inward_main("D", 0)
                    inward_tail("D", 0)
                    met_z("N")
                    inward_main("N", 0)
                    inward_tail("N", 0)
                    inward_main("C", 1)
                    inward_tail("C", 1)
                    inward_main("D", 1)
                    inward_tail("D", 1)
                    inward_main("N", 1)
                    inward_tail("N", 1)

                @pl.when(jnp.logical_not(core == 0))
                def _():
                    met_z("C")
                    inward_main("C", 0)
                    inward_tail("C", 0)
                    met_z("D")
                    inward_main("D", 0)
                    inward_tail("D", 0)
                    met_z("N")
                    inward_main("N", 0)
                    inward_tail("N", 0)
                    inward_main("C", 1)
                    inward_tail("C", 1)
                    inward_main("D", 1)
                    inward_tail("D", 1)
                    inward_main("N", 1)
                    inward_tail("N", 1)


            @pl.when(jnp.logical_not(z == 2))
            def _():

                @pl.when(core == 0)
                def _():
                    met_z("N")
                    inward_main("N", 0)
                    inward_tail("N", 0)
                    met_z("C")
                    inward_main("C", 0)
                    inward_tail("C", 0)
                    met_z("D")
                    inward_main("D", 0)
                    inward_tail("D", 0)
                    inward_main("N", 1)
                    inward_tail("N", 1)
                    inward_main("C", 1)
                    inward_tail("C", 1)
                    inward_main("D", 1)
                    inward_tail("D", 1)

                @pl.when(jnp.logical_not(core == 0))
                def _():
                    met_z("N")
                    inward_main("N", 0)
                    inward_tail("N", 0)
                    met_z("C")
                    inward_main("C", 0)
                    inward_tail("C", 0)
                    met_z("D")
                    inward_main("D", 0)
                    inward_tail("D", 0)
                    inward_main("N", 1)
                    inward_tail("N", 1)
                    inward_main("C", 1)
                    inward_tail("C", 1)
                    inward_main("D", 1)
                    inward_tail("D", 1)


        @pl.when(jnp.logical_not(inner))
        def _():
            met_z("C")
            inward_main("C", 0)
            inward_tail("C", 0)

        met_way(1)
        direct_main(0, 1)
        direct_tail(0, 1)
        direct_main(1, 1)
        direct_tail(1, 1)


    @pl.when(chip == 3)
    def _():

        @pl.when(inner)
        def _():

            @pl.when(z == 2)
            def _():

                @pl.when(core == 0)
                def _():
                    met_z("C")
                    inward_main("C", 0)
                    inward_tail("C", 0)
                    met_z("D")
                    inward_main("D", 0)
                    inward_tail("D", 0)
                    met_z("N")
                    inward_main("N", 0)
                    inward_tail("N", 0)
                    inward_main("C", 1)
                    inward_tail("C", 1)
                    inward_main("D", 1)
                    inward_tail("D", 1)
                    inward_main("N", 1)
                    inward_tail("N", 1)

                @pl.when(jnp.logical_not(core == 0))
                def _():
                    met_z("C")
                    inward_main("C", 0)
                    inward_tail("C", 0)
                    met_z("D")
                    inward_main("D", 0)
                    inward_tail("D", 0)
                    met_z("N")
                    inward_main("N", 0)
                    inward_tail("N", 0)
                    inward_main("C", 1)
                    inward_tail("C", 1)
                    inward_main("D", 1)
                    inward_tail("D", 1)
                    inward_main("N", 1)
                    inward_tail("N", 1)


            @pl.when(jnp.logical_not(z == 2))
            def _():

                @pl.when(core == 0)
                def _():
                    met_z("N")
                    inward_main("N", 0)
                    inward_tail("N", 0)
                    met_z("C")
                    inward_main("C", 0)
                    inward_tail("C", 0)
                    met_z("D")
                    inward_main("D", 0)
                    inward_tail("D", 0)
                    inward_main("N", 1)
                    inward_tail("N", 1)
                    inward_main("C", 1)
                    inward_tail("C", 1)
                    inward_main("D", 1)
                    inward_tail("D", 1)

                @pl.when(jnp.logical_not(core == 0))
                def _():
                    met_z("N")
                    inward_main("N", 0)
                    inward_tail("N", 0)
                    met_z("C")
                    inward_main("C", 0)
                    inward_tail("C", 0)
                    met_z("D")
                    inward_main("D", 0)
                    inward_tail("D", 0)
                    inward_main("N", 1)
                    inward_tail("N", 1)
                    inward_main("C", 1)
                    inward_tail("C", 1)
                    inward_main("D", 1)
                    inward_tail("D", 1)


        @pl.when(jnp.logical_not(inner))
        def _():
            inward_tail("N", 0)
            met_z("C")
            inward_main("C", 0)
            inward_tail("C", 0)
            met_z("D")
            inward_main("D", 0)
            inward_tail("D", 0)
            inward_main("N", 1)
            inward_tail("N", 1)
            inward_main("C", 1)
            inward_tail("C", 1)
            inward_main("D", 1)
            inward_tail("D", 1)


    @pl.when(jnp.logical_not(chip == 3))
    def _():

        @pl.when(jnp.logical_not(inner))
        def _():
            met_z("D")
            inward_main("D", 0)
            inward_tail("D", 0)
            inward_main("N", 1)
            inward_tail("N", 1)
            inward_main("C", 1)
            inward_tail("C", 1)
            inward_main("D", 1)
            inward_tail("D", 1)


    met(0)
    send(vpairs_hbm, other_pairs, pair_send.at[0], pair_recv.at[0], partner)
    send(ints_hbm, other_ints, pair_send.at[1], pair_recv.at[1], partner)
    for b in range(blocks_here):
        gath[b, z, chip, bulk:chunk] = tails[b]
    for load in rest:
        load.wait()

    occ_column = as_column(occ_e[...].reshape(1, -1))
    occ_row = picked_row(occ_column, opairs[0:1, :]) + picked_row(occ_column, opairs[1:2, :])
    occ_col[...] = jnp.broadcast_to(as_column(occ_row), occ_col.shape)
    virt_column = as_column(virt_e[...].reshape(1, -1))

    def prepare(side, int_ref, pair_ref):
        for b in range(blocks_here):
            virt_row = picked_row(virt_column, pair_ref[b, 0:1, :]) + picked_row(
                virt_column, pair_ref[b, 1:2, :]
            )
            for p in range(gath.shape[2]):
                start = pl.multiple_of((2 * p + core) * nij, 8)
                occ = occ_col[pl.ds(start, nij), 0:1]
                recip[b, side, p] = 1.0 / (occ - virt_row)
            for zz in range(groups):
                panel = int_ref[b, :, zz * nef : (zz + 1) * nef].astype(F32)
                last = panel[:, main:nef]
                wide = jnp.concatenate([panel[:, 0:main], last, last], axis=1)
                width = main + LANES
                weights[b, side, :, zz * width : (zz + 1) * width] = wide.astype(BF16)

    lane = lax.broadcasted_iota(jnp.int32, (half, LANES), 1)
    main_lanes = nab // LANES * LANES

    def job(b, *columns):
        panels = []
        for p in columns:
            parts = []
            for zz in range(groups):
                end = gath[b, zz, p, bulk:chunk]
                zero = jnp.zeros_like(end)
                end2 = jnp.concatenate(
                    [jnp.where(lane < tail, end, zero), jnp.where(lane < tail, zero, end)], axis=0
                )
                parts += [gath[b, zz, p, i * rows : (i + 1) * rows] for i in range(main // LANES)] + [end2]
            panels.append(jnp.concatenate(parts, axis=1))
        panel = jnp.concatenate(panels, axis=0)
        for side in range(2):
            total = lax.dot_general(
                panel, weights[b, side], (((1,), (1,)), ((), ())), preferred_element_type=F32
            )
            for i, p in enumerate(columns):
                scaled = total[i * rows : (i + 1) * rows].reshape(vec, nij, nab) * recip[b, side, p][None]
                ends = [scaled[v, :, main_lanes:nab] for v in range(vec)]
                sendbuf[b, p, side, 0:rows, :] = scaled[:, :, 0:main_lanes].reshape(rows, main_lanes).astype(BF16)
                sendbuf[b, p, side, rows : rows + nij, :] = jnp.concatenate(ends, axis=1).astype(BF16)
        for p in columns:
            deliver(b, p)

    def deliver(b, p):
        @pl.when(p != z)
        def _():
            for side in range(2):
                send(
                    sendbuf.at[b, p, side], recvbuf.at[z, b, core], o_send.at[0], o_recv.at[z, b],
                    at(p, chip, core if side == 0 else 1 - core),
                )

        @pl.when(p == z)
        def _():
            send(sendbuf.at[b, z, 1], recvbuf.at[z, b, core], o_send.at[1], o_recv.at[z, b], partner)
            recvbuf[z, b, core] = sendbuf[b, z, 0]

    wanted = [far(s) for s in range(groups - 1)] + [z]
    spot = sum(jnp.where(wanted[i] == diag, i, 0) for i in range(groups))
    late = [jnp.where(i >= spot, wanted[i + 1], wanted[i]) for i in range(groups - 1)] + [diag]

    def unpack(zz, b):
        got = [recvbuf[zz, b, c].astype(F32) for c in range(2)]
        width = nab - main_lanes
        for v in range(vec):
            pieces = []
            for c in range(2):
                body_rows = got[c][v * nij : (v + 1) * nij, :]
                end = got[c][rows : rows + nij, v * width : (v + 1) * width]
                pieces.append(jnp.concatenate([body_rows, end], axis=1))
            out[zz * blocks_here + b, v] = jnp.concatenate(pieces, axis=0).astype(BF16)

    second("O", 0)
    prepare(0, ints, vpairs)
    first("N", 0)
    arrived(other_pairs, pair_recv.at[0])
    arrived(other_ints, pair_recv.at[1])
    prepare(1, other_ints, other_pairs)
    second("O", 1)

    @pl.when(inner)
    def _():
        first("E", 0)
        first("G", 0)
        second("N", 0)
        second("E", 0)
        first("N", 1)
        first("E", 1)
        second("G", 0)
        met(len(peers) - 1)
        first("G", 1)
        cross("G", 1)

    @pl.when(jnp.logical_not(inner))
    def _():

        @pl.when(core == 0)
        def _():
            first("N", 1)
            second("N", 0)
            first("E", 0)
            second("N", 1)
            first("G", 0)
            first("E", 1)
            second("E", 0)
            second("G", 0)
            met(len(peers) - 1)
            first("G", 1)
            cross("G", 1)

        @pl.when(jnp.logical_not(core == 0))
        def _():
            first("N", 1)
            second("N", 0)
            second("N", 1)
            first("E", 0)
            first("G", 0)
            second("E", 0)
            first("E", 1)
            second("G", 0)
            met(len(peers) - 1)
            first("G", 1)
            cross("G", 1)


    pltpu.make_async_copy(gath.at[:, z, chip, 0:bulk], gath.at[:, z, chip, 0:bulk], load_own.at[0]).wait()
    for s in range(groups - 1):
        met(4 + 2 * s)
    job(0, late[0], late[1])
    second("E", 1)

    @pl.when(inner)
    def _():
        second("N", 1)

    job(0, late[2])
    third(0)
    job(0, late[3])
    settled("G", 1)
    job(1, late[0], late[1], late[2])
    third(1)
    job(1, late[3])

    for b in range(blocks_here):
        arrived(recvbuf.at[z, b, 1 - core], o_recv.at[z, b])
        unpack(z, b)
        for s in range(groups - 1):
            zz = far(s)
            arrived(recvbuf.at[zz, b], o_recv.at[zz, b])
            unpack(zz, b)
    left(gath.at[:, 0 : groups - 1, 0], z_send.at[0])
    left(gath.at[0], d_send.at[0])
    left(gath.at[:, :, 0], f_send.at[0])
    left(sendbuf.at[:, 0 : groups - 1], o_send.at[0])
    left(sendbuf.at[:, 0, 0], o_send.at[1])
    left(other_pairs, pair_send.at[0])
    left(other_ints, pair_send.at[1])


def fused(groups, integrals, amplitudes, occupied_energy, virtual_energy, virtual_pairs, occupied_pairs):
    nblk, nef, vec, nij = amplitudes.shape
    here, nab, _ = integrals.shape
    rows = vec * nij
    chips = lax.axis_size("dev") // 2
    amps = jnp.transpose(amplitudes, (0, 2, 3, 1)).reshape(nblk, rows, nef)
    vpairs = jnp.transpose(virtual_pairs, (0, 2, 1))
    opairs = jnp.transpose(occupied_pairs, (1, 0))
    dims = (groups, here, vec, nij, nab, nef)
    dma = pltpu.SemaphoreType.DMA
    arrays = (integrals, amps, occupied_energy, virtual_energy, vpairs, opairs)
    result = pl.pallas_call(
        functools.partial(body, dims),
        out_shape=jax.ShapeDtypeStruct((nblk, vec, 2 * nij, nab), BF16),
        in_specs=[pl.BlockSpec(memory_space=pltpu.HBM)] * 6,
        out_specs=pl.BlockSpec(memory_space=pltpu.VMEM),
        scratch_shapes=[
            pltpu.VMEM(integrals.shape, BF16),
            pltpu.VMEM(amps.shape, BF16),
            pltpu.VMEM(occupied_energy.shape, F32),
            pltpu.VMEM(virtual_energy.shape, F32),
            pltpu.VMEM(vpairs.shape, jnp.int32),
            pltpu.VMEM(opairs.shape, jnp.int32),
            pltpu.VMEM((nblk, rows // 2, LANES), BF16),
            pltpu.VMEM((here, groups, chips, 2 * rows + rows // 2, LANES), BF16),
            pltpu.VMEM(integrals.shape, BF16),
            pltpu.VMEM(vpairs.shape, jnp.int32),
            pltpu.VMEM((here, 2, nab, groups * 3 * LANES), BF16),
            pltpu.VMEM((here, 2, chips, nij, nab), F32),
            pltpu.VMEM((2 * chips * nij, LANES), F32),
            pltpu.VMEM((here, groups, 2, rows + nij, LANES), BF16),
            pltpu.VMEM((groups, here, 2, rows + nij, LANES), BF16),
            pltpu.SemaphoreType.REGULAR((4 + 2 * (groups - 1),)),
            dma((1,)),
            dma((here, groups)),
            dma((1,)),
            dma((here, groups)),
            dma((1,)),
            dma((here,)),
            dma((2,)),
            dma((groups, here)),
            dma((2,)),
            dma((2,)),
            dma((2,)),
            dma((1,)),
            dma((5,)),
        ],
        compiler_params=pltpu.CompilerParams(
            collective_id=0, has_side_effects=True, vmem_limit_bytes=32 * 1024 * 1024
        ),
        name="ladder",
    )(*[pltpu.with_memory_space_constraint(array, pltpu.HBM) for array in arrays])
    return jnp.transpose(result, (0, 3, 1, 2))


def solution(mesh):
    placed = (
        P("grp", "dev", None),
        P(None, "grp", None, "dev"),
        P(),
        P(),
        P("grp", "dev", None),
        P(),
    )
    groups, devs = mesh.shape["grp"], mesh.shape["dev"]

    def local(integrals, amplitudes, *rest):
        nef, vec, nij = amplitudes.shape[1:]
        nab = integrals.shape[1]
        square = devs == 2 * 2 * 2 and devs == 2 * groups
        packs = (
            2 * LANES < nef < 3 * LANES
            and 2 * (nef % LANES) == LANES
            and LANES < nab < 2 * LANES
            and vec * (nab % LANES) == LANES
            and nij % 8 == 0
            and (vec * nij) % 32 == 0
        )
        if square and packs:
            return fused(groups, integrals, amplitudes, *rest)
        return plain(integrals, amplitudes, *rest)

    return jax.shard_map(
        local, mesh=mesh, in_specs=placed, out_specs=P(None, "dev", None, "grp"), check_vma=False
    )
```

```python
import functools

import jax
import jax.numpy as jnp
from jax import lax
from jax.experimental import pallas as pl
from jax.experimental.pallas import tpu as pltpu
from jax.sharding import PartitionSpec as P

LANES = 128
F32 = jnp.float32
BF16 = jnp.bfloat16


def lookup(energy, indices):
    labels = jnp.arange(energy.shape[0], dtype=jnp.int32)
    picked = indices[:, None] == labels[None, :]
    return jnp.sum(jnp.where(picked, energy[None, :], 0.0), axis=1)


def plain(integrals, amplitudes, occupied_energy, virtual_energy, virtual_pairs, occupied_pairs):
    arrived = lax.all_to_all(amplitudes, "grp", split_axis=0, concat_axis=1, tiled=True)
    occ_sum = lookup(occupied_energy, occupied_pairs[:, 0]) + lookup(
        occupied_energy, occupied_pairs[:, 1]
    )
    results = []
    for block in range(arrived.shape[0]):
        panel = arrived[block]
        block_ints = integrals[block]
        gathered = lax.all_gather(panel, "dev", axis=2, tiled=True)
        ladder = jnp.einsum("ae,evj->avj", block_ints, gathered, preferred_element_type=jnp.float32)
        pairs_here = virtual_pairs[block]
        virt_sum = lookup(virtual_energy, pairs_here[:, 0]) + lookup(
            virtual_energy, pairs_here[:, 1]
        )
        denominator = occ_sum[None, :] - virt_sum[:, None]
        results.append((ladder / denominator[:, None, :]).astype(jnp.bfloat16))
    stacked = jnp.stack(results)
    return lax.all_to_all(stacked, "grp", split_axis=3, concat_axis=0, tiled=True)


def as_column(row):
    n = row.shape[1]
    eye = lax.broadcasted_iota(jnp.int32, (n, n), 0) == lax.broadcasted_iota(jnp.int32, (n, n), 1)
    return jnp.sum(jnp.where(eye, jnp.broadcast_to(row, (n, n)), 0.0), axis=1, keepdims=True)


def picked_row(column, index_row):
    shape = (column.shape[0], index_row.shape[1])
    hit = lax.broadcasted_iota(jnp.int32, shape, 0) == jnp.broadcast_to(index_row, shape)
    return jnp.sum(jnp.where(hit, jnp.broadcast_to(column, shape), 0.0), axis=0, keepdims=True)


def body(
    dims,
    ints_hbm,
    amps_hbm,
    occ_e_hbm,
    virt_e_hbm,
    vpairs_hbm,
    opairs_hbm,
    out,
    ints,
    amps,
    occ_e,
    virt_e,
    vpairs,
    opairs,
    tails,
    gath,
    other_ints,
    other_pairs,
    weights,
    recip,
    occ_col,
    sendbuf,
    recvbuf,
    ready,
    z_send,
    z_recv,
    d_send,
    d_recv,
    f_recv,
    o_send,
    o_recv,
    pair_send,
    pair_recv,
    load_amps,
    load_own,
    load_rest,
):
    groups, blocks_here, vec, nij, nab, nef = dims
    rows = vec * nij
    half = rows // 2
    tail = nef % LANES
    main = nef - tail
    bulk = main // LANES * rows
    chunk = bulk + half
    cut = chunk // 32 * 16
    z = lax.axis_index("grp")
    dev = lax.axis_index("dev")
    core = dev % 2
    chip = dev // 2
    flip_x = chip + 1 - 2 * (chip % 2)
    flip_y = chip + 2 - 4 * (chip // 2)
    diag = 3 - chip
    mesh_id = pl.DeviceIdType.MESH

    def at(zz, pp, cc):
        return (zz, pp * 2 + cc)

    low = z < groups // 2

    def far(step):
        down = groups - 1 - step
        down = down - jnp.where(down <= z, 1, 0)
        up = step + jnp.where(step >= z, 1, 0)
        return jnp.where(low, down, up)

    def across(step):
        return jnp.where(low, groups // 2 + step, groups // 2 - 1 - step)

    def reach(step):
        return jnp.where(step < z, z - 1 - step, step + 1)

    loads = []
    for b in range(blocks_here):
        loads.append(pltpu.make_async_copy(amps_hbm.at[z * blocks_here + b], amps.at[b], load_amps.at[0]))
    for s in range(groups - 1):
        for b in range(blocks_here):
            slot = (s + 1) * blocks_here + b
            loads.append(
                pltpu.make_async_copy(amps_hbm.at[reach(s) * blocks_here + b], amps.at[slot], load_amps.at[1])
            )

    def bulk_parts(block, piece):
        for i in range(main // LANES):
            yield amps_hbm.at[block, :, i * LANES : (i + 1) * LANES], piece.at[i * rows : (i + 1) * rows]

    for b in range(blocks_here):
        for src, dst in bulk_parts(z * blocks_here + b, gath.at[b, z, chip]):
            loads.append(pltpu.make_async_copy(src, dst, load_own.at[0]))
    pairs = [(ints_hbm, ints), (occ_e_hbm, occ_e), (virt_e_hbm, virt_e), (vpairs_hbm, vpairs), (opairs_hbm, opairs)]
    rest = [pltpu.make_async_copy(src, dst, load_rest.at[i]) for i, (src, dst) in enumerate(pairs)]

    partner = at(z, chip, 1 - core)
    x_peer = at(z, flip_x, core)
    y_peer = at(z, flip_y, core)
    swap = chip == 2
    ways = [
        at(z, jnp.where(swap, flip_y, flip_x), core),
        at(z, jnp.where(swap, flip_x, flip_y), core),
    ]
    peers = [(partner, core == 0, 0), (x_peer, chip % 2 == 0, 1), (y_peer, chip < 2, 2)]
    last = 3 + groups - 1
    for s in range(groups - 1):
        zz = reach(s)
        peers.append((at(zz, chip, core), zz > z, 3 + s))
    d_peer = at(z, diag, core)
    peers.append((d_peer, chip < 2, last))
    barrier = pltpu.get_barrier_semaphore()
    for peer, higher, _ in peers:
        @pl.when(higher)
        def _(peer=peer):
            pl.semaphore_signal(barrier, inc=1, device_id=peer, device_id_type=mesh_id)
    for load in loads + rest:
        load.start()
    earlier = z + chip + core

    @pl.when(earlier > 0)
    def _():
        pl.semaphore_wait(barrier, earlier)

    for i, (peer, higher, slot) in enumerate(peers):
        if i < 3 or slot == last:
            there = slot
        else:
            zz = reach(i - 3)
            there = 3 + jnp.where(z < zz, zz - 1 - z, z - 1)

        @pl.when(jnp.logical_not(higher))
        def _(peer=peer, there=there):
            pl.semaphore_signal(ready.at[there], inc=1, device_id=peer, device_id_type=mesh_id)

    def met_z(name):
        spot = outlets[name][1]
        higher = outlets[name][0] > z

        @pl.when(higher)
        def _():
            pl.semaphore_wait(ready.at[3 + spot], 1)

    def met(i):
        @pl.when(peers[i][1])
        def _():
            pl.semaphore_wait(ready.at[peers[i][2]], 1)

    def met_way(way):
        i = jnp.where(swap, 2 - way, 1 + way)
        higher = jnp.where(i == 1, chip % 2 == 0, chip < 2)

        @pl.when(higher)
        def _():
            pl.semaphore_wait(ready.at[i], 1)

    def send(src, dst, ssem, rsem, to):
        pltpu.make_async_remote_copy(
            src_ref=src, dst_ref=dst, send_sem=ssem, recv_sem=rsem, device_id=to, device_id_type=mesh_id
        ).start()

    def whole(ref, sem):
        return pltpu.make_async_remote_copy(
            src_ref=ref, dst_ref=ref, send_sem=sem, recv_sem=sem, device_id=partner, device_id_type=mesh_id
        )

    def arrived(ref, sem):
        whole(ref, sem).wait_recv()

    def left(ref, sem):
        whole(ref, sem).wait_send()

    near = z + 1 - 2 * (z % 2)
    inner = jnp.logical_and(z > 0, z < groups - 1)
    sources = {"O": (z, z), "N": (near, near), "C": (across(0),) * 2, "D": (across(1),) * 2}
    turn = [
        jnp.where(jnp.logical_or(z == groups - 1, jnp.logical_and(core == 0, z != 1)), 1, 0),
        jnp.where(jnp.logical_and(core == 1, z == 1), 0, 1),
    ]
    sources["E"] = tuple(across(t) for t in turn)
    sources["G"] = tuple(across(1 - t) for t in turn)

    def direct_main(b, way):
        for src, dst in bulk_parts(z * blocks_here + b, gath.at[b, z, chip]):
            send(src, dst, d_send.at[0], d_recv.at[b, z], ways[way])

    def direct_tail(b, way):
        send(tails.at[b], gath.at[b, z, chip, bulk:chunk], d_send.at[0], d_recv.at[b, z], ways[way])

    skip = jnp.where(z == 2, 0, 1)
    outlets = {"N": (near, 2 * (1 - skip)), "C": (across(0), skip), "D": (across(1), skip + 1)}

    def inward_main(name, b):
        to = outlets[name][0]
        for src, dst in bulk_parts(to * blocks_here + b, gath.at[b, z, chip]):
            send(src, dst, z_send.at[0], z_recv.at[b, z], at(to, chip, core))

    def inward_tail(name, b):
        to, spot = outlets[name]
        send(
            tails.at[(spot + 1) * blocks_here + b], gath.at[b, z, chip, bulk:chunk],
            z_send.at[0], z_recv.at[b, z], at(to, chip, core),
        )

    def first(name, b):
        zz = sources[name][b]
        piece = gath.at[b, zz, chip]
        arrived(piece, z_recv.at[b, zz])
        for peer in (x_peer, y_peer):
            send(piece, piece, d_send.at[0], d_recv.at[b, zz], peer)

    def second(name, b):
        zz = sources[name][b]
        arrived(gath.at[b, zz, 0:2], d_recv.at[b, zz])
        src = gath.at[b, zz, flip_x, 0:cut]
        send(src, src, d_send.at[0], f_recv.at[b], y_peer)
        src = gath.at[b, zz, flip_y, cut:chunk]
        send(src, src, d_send.at[0], f_recv.at[b], x_peer)

    def cross(name, b):
        piece = gath.at[b, sources[name][b], chip]
        send(piece, piece, d_send.at[0], f_recv.at[b], d_peer)

    def settled(name, b):
        arrived(gath.at[b, sources[name][b], 0:2], d_recv.at[b, sources[name][b]])

    def third(b):
        arrived(gath.at[b, :, diag], f_recv.at[b])

    def pack(slot):
        lower = amps[slot, 0:half, main:nef].astype(F32)
        upper = amps[slot, half:rows, main:nef].astype(F32)
        tails[slot] = jnp.concatenate([lower, upper], axis=1).astype(BF16)

    def loaded(slots, sem):
        pltpu.make_async_copy(amps.at[slots], amps.at[slots], sem).wait()


    @pl.when(chip == 3)
    def _():
        met_way(0)
        direct_main(0, 0)
        met_way(1)
        direct_main(0, 1)

        @pl.when(jnp.logical_not(inner))
        def _():
            met_z("N")
            inward_main("N", 0)

        loaded(slice(0, blocks_here), load_amps.at[0])
        for b in range(blocks_here):
            pack(b)
        direct_tail(0, 0)
        direct_tail(0, 1)
        direct_main(1, 0)
        direct_main(1, 1)
        direct_tail(1, 0)
        direct_tail(1, 1)
        loaded(slice(blocks_here, groups * blocks_here), load_amps.at[1])
        for slot in range(blocks_here, groups * blocks_here):
            pack(slot)

    @pl.when(jnp.logical_not(chip == 3))
    def _():

        @pl.when(jnp.logical_not(chip == 0))
        def _():
            met_way(0)
            direct_main(0, 0)


        @pl.when(jnp.logical_not(inner))
        def _():
            met_z("N")
            inward_main("N", 0)

        loaded(slice(0, blocks_here), load_amps.at[0])
        for b in range(blocks_here):
            pack(b)
        loaded(slice(blocks_here, groups * blocks_here), load_amps.at[1])
        for slot in range(blocks_here, groups * blocks_here):
            pack(slot)

        @pl.when(chip == 0)
        def _():
            met_way(0)
            direct_main(0, 0)


        @pl.when(jnp.logical_not(inner))
        def _():
            inward_tail("N", 0)

        direct_tail(0, 0)
        direct_main(1, 0)
        direct_tail(1, 0)

        @pl.when(inner)
        def _():

            @pl.when(z == 2)
            def _():

                @pl.when(core == 0)
                def _():
                    met_z("C")
                    inward_main("C", 0)
                    inward_tail("C", 0)
                    met_z("D")
                    inward_main("D", 0)
                    inward_tail("D", 0)
                    met_z("N")
                    inward_main("N", 0)
                    inward_tail("N", 0)
                    inward_main("C", 1)
                    inward_tail("C", 1)
                    inward_main("D", 1)
                    inward_tail("D", 1)
                    inward_main("N", 1)
                    inward_tail("N", 1)

                @pl.when(jnp.logical_not(core == 0))
                def _():
                    met_z("C")
                    inward_main("C", 0)
                    inward_tail("C", 0)
                    met_z("D")
                    inward_main("D", 0)
                    inward_tail("D", 0)
                    met_z("N")
                    inward_main("N", 0)
                    inward_tail("N", 0)
                    inward_main("C", 1)
                    inward_tail("C", 1)
                    inward_main("D", 1)
                    inward_tail("D", 1)
                    inward_main("N", 1)
                    inward_tail("N", 1)


            @pl.when(jnp.logical_not(z == 2))
            def _():

                @pl.when(core == 0)
                def _():
                    met_z("N")
                    inward_main("N", 0)
                    inward_tail("N", 0)
                    met_z("C")
                    inward_main("C", 0)
                    inward_tail("C", 0)
                    met_z("D")
                    inward_main("D", 0)
                    inward_tail("D", 0)
                    inward_main("N", 1)
                    inward_tail("N", 1)
                    inward_main("C", 1)
                    inward_tail("C", 1)
                    inward_main("D", 1)
                    inward_tail("D", 1)

                @pl.when(jnp.logical_not(core == 0))
                def _():
                    met_z("N")
                    inward_main("N", 0)
                    inward_tail("N", 0)
                    met_z("C")
                    inward_main("C", 0)
                    inward_tail("C", 0)
                    met_z("D")
                    inward_main("D", 0)
                    inward_tail("D", 0)
                    inward_main("N", 1)
                    inward_tail("N", 1)
                    inward_main("C", 1)
                    inward_tail("C", 1)
                    inward_main("D", 1)
                    inward_tail("D", 1)


        @pl.when(jnp.logical_not(inner))
        def _():
            met_z("C")
            inward_main("C", 0)
            inward_tail("C", 0)

        met_way(1)
        direct_main(0, 1)
        direct_tail(0, 1)
        direct_main(1, 1)
        direct_tail(1, 1)


    @pl.when(chip == 3)
    def _():

        @pl.when(inner)
        def _():

            @pl.when(z == 2)
            def _():

                @pl.when(core == 0)
                def _():
                    met_z("C")
                    inward_main("C", 0)
                    inward_tail("C", 0)
                    met_z("D")
                    inward_main("D", 0)
                    inward_tail("D", 0)
                    met_z("N")
                    inward_main("N", 0)
                    inward_tail("N", 0)
                    inward_main("C", 1)
                    inward_tail("C", 1)
                    inward_main("D", 1)
                    inward_tail("D", 1)
                    inward_main("N", 1)
                    inward_tail("N", 1)

                @pl.when(jnp.logical_not(core == 0))
                def _():
                    met_z("C")
                    inward_main("C", 0)
                    inward_tail("C", 0)
                    met_z("D")
                    inward_main("D", 0)
                    inward_tail("D", 0)
                    met_z("N")
                    inward_main("N", 0)
                    inward_tail("N", 0)
                    inward_main("C", 1)
                    inward_tail("C", 1)
                    inward_main("D", 1)
                    inward_tail("D", 1)
                    inward_main("N", 1)
                    inward_tail("N", 1)


            @pl.when(jnp.logical_not(z == 2))
            def _():

                @pl.when(core == 0)
                def _():
                    met_z("N")
                    inward_main("N", 0)
                    inward_tail("N", 0)
                    met_z("C")
                    inward_main("C", 0)
                    inward_tail("C", 0)
                    met_z("D")
                    inward_main("D", 0)
                    inward_tail("D", 0)
                    inward_main("N", 1)
                    inward_tail("N", 1)
                    inward_main("C", 1)
                    inward_tail("C", 1)
                    inward_main("D", 1)
                    inward_tail("D", 1)

                @pl.when(jnp.logical_not(core == 0))
                def _():
                    met_z("N")
                    inward_main("N", 0)
                    inward_tail("N", 0)
                    met_z("C")
                    inward_main("C", 0)
                    inward_tail("C", 0)
                    met_z("D")
                    inward_main("D", 0)
                    inward_tail("D", 0)
                    inward_main("N", 1)
                    inward_tail("N", 1)
                    inward_main("C", 1)
                    inward_tail("C", 1)
                    inward_main("D", 1)
                    inward_tail("D", 1)


        @pl.when(jnp.logical_not(inner))
        def _():
            inward_tail("N", 0)
            met_z("C")
            inward_main("C", 0)
            inward_tail("C", 0)
            met_z("D")
            inward_main("D", 0)
            inward_tail("D", 0)
            inward_main("N", 1)
            inward_tail("N", 1)
            inward_main("C", 1)
            inward_tail("C", 1)
            inward_main("D", 1)
            inward_tail("D", 1)


    @pl.when(jnp.logical_not(chip == 3))
    def _():

        @pl.when(jnp.logical_not(inner))
        def _():
            met_z("D")
            inward_main("D", 0)
            inward_tail("D", 0)
            inward_main("N", 1)
            inward_tail("N", 1)
            inward_main("C", 1)
            inward_tail("C", 1)
            inward_main("D", 1)
            inward_tail("D", 1)


    met(0)
    send(vpairs_hbm, other_pairs, pair_send.at[0], pair_recv.at[0], partner)
    send(ints_hbm, other_ints, pair_send.at[1], pair_recv.at[1], partner)
    for b in range(blocks_here):
        gath[b, z, chip, bulk:chunk] = tails[b]
    for load in rest:
        load.wait()

    occ_column = as_column(occ_e[...].reshape(1, -1))
    occ_row = picked_row(occ_column, opairs[0:1, :]) + picked_row(occ_column, opairs[1:2, :])
    occ_col[...] = jnp.broadcast_to(as_column(occ_row), occ_col.shape)
    virt_column = as_column(virt_e[...].reshape(1, -1))

    def prepare(side, int_ref, pair_ref):
        for b in range(blocks_here):
            virt_row = picked_row(virt_column, pair_ref[b, 0:1, :]) + picked_row(
                virt_column, pair_ref[b, 1:2, :]
            )
            for p in range(gath.shape[2]):
                start = pl.multiple_of((2 * p + core) * nij, 8)
                occ = occ_col[pl.ds(start, nij), 0:1]
                recip[b, side, p] = 1.0 / (occ - virt_row)
            for zz in range(groups):
                panel = int_ref[b, :, zz * nef : (zz + 1) * nef].astype(F32)
                last = panel[:, main:nef]
                wide = jnp.concatenate([panel[:, 0:main], last, last], axis=1)
                width = main + LANES
                weights[b, side, :, zz * width : (zz + 1) * width] = wide.astype(BF16)

    lane = lax.broadcasted_iota(jnp.int32, (half, LANES), 1)
    main_lanes = nab // LANES * LANES

    def job(b, *columns):
        panels = []
        for p in columns:
            parts = []
            for zz in range(groups):
                end = gath[b, zz, p, bulk:chunk]
                zero = jnp.zeros_like(end)
                end2 = jnp.concatenate(
                    [jnp.where(lane < tail, end, zero), jnp.where(lane < tail, zero, end)], axis=0
                )
                parts += [gath[b, zz, p, i * rows : (i + 1) * rows] for i in range(main // LANES)] + [end2]
            panels.append(jnp.concatenate(parts, axis=1))
        panel = jnp.concatenate(panels, axis=0)
        for side in range(2):
            total = lax.dot_general(
                panel, weights[b, side], (((1,), (1,)), ((), ())), preferred_element_type=F32
            )
            for i, p in enumerate(columns):
                scaled = total[i * rows : (i + 1) * rows].reshape(vec, nij, nab) * recip[b, side, p][None]
                ends = [scaled[v, :, main_lanes:nab] for v in range(vec)]
                sendbuf[b, p, side, 0:rows, :] = scaled[:, :, 0:main_lanes].reshape(rows, main_lanes).astype(BF16)
                sendbuf[b, p, side, rows : rows + nij, :] = jnp.concatenate(ends, axis=1).astype(BF16)
        for p in columns:
            deliver(b, p)

    def deliver(b, p):
        @pl.when(p != z)
        def _():
            for side in range(2):
                send(
                    sendbuf.at[b, p, side], recvbuf.at[z, b, core], o_send.at[0], o_recv.at[z, b],
                    at(p, chip, core if side == 0 else 1 - core),
                )

        @pl.when(p == z)
        def _():
            send(sendbuf.at[b, z, 1], recvbuf.at[z, b, core], o_send.at[1], o_recv.at[z, b], partner)
            recvbuf[z, b, core] = sendbuf[b, z, 0]

    wanted = [far(s) for s in range(groups - 1)] + [z]
    spot = sum(jnp.where(wanted[i] == diag, i, 0) for i in range(groups))
    late = [jnp.where(i >= spot, wanted[i + 1], wanted[i]) for i in range(groups - 1)] + [diag]

    def unpack(zz, b):
        got = [recvbuf[zz, b, c].astype(F32) for c in range(2)]
        width = nab - main_lanes
        for v in range(vec):
            pieces = []
            for c in range(2):
                body_rows = got[c][v * nij : (v + 1) * nij, :]
                end = got[c][rows : rows + nij, v * width : (v + 1) * width]
                pieces.append(jnp.concatenate([body_rows, end], axis=1))
            out[zz * blocks_here + b, v] = jnp.concatenate(pieces, axis=0).astype(BF16)

    second("O", 0)
    prepare(0, ints, vpairs)
    first("N", 0)
    arrived(other_pairs, pair_recv.at[0])
    arrived(other_ints, pair_recv.at[1])
    prepare(1, other_ints, other_pairs)
    second("O", 1)

    @pl.when(inner)
    def _():
        first("E", 0)
        first("G", 0)
        second("N", 0)
        second("E", 0)
        first("N", 1)
        first("E", 1)
        second("G", 0)
        met(len(peers) - 1)
        first("G", 1)
        cross("G", 1)

    @pl.when(jnp.logical_not(inner))
    def _():

        @pl.when(core == 0)
        def _():
            first("N", 1)
            second("N", 0)
            first("E", 0)
            second("N", 1)
            first("G", 0)
            first("E", 1)
            second("E", 0)
            second("G", 0)
            met(len(peers) - 1)
            first("G", 1)
            cross("G", 1)

        @pl.when(jnp.logical_not(core == 0))
        def _():
            first("N", 1)
            second("N", 0)
            second("N", 1)
            first("E", 0)
            first("G", 0)
            second("E", 0)
            first("E", 1)
            second("G", 0)
            met(len(peers) - 1)
            first("G", 1)
            cross("G", 1)


    pltpu.make_async_copy(gath.at[:, z, chip, 0:bulk], gath.at[:, z, chip, 0:bulk], load_own.at[0]).wait()
    job(0, late[0], late[1])
    second("E", 1)

    @pl.when(inner)
    def _():
        second("N", 1)

    job(0, late[2])
    third(0)
    job(0, late[3])
    settled("G", 1)
    job(1, late[0], late[1], late[2])
    third(1)
    job(1, late[3])

    for b in range(blocks_here):
        arrived(recvbuf.at[z, b, 1 - core], o_recv.at[z, b])
        unpack(z, b)
        for s in range(groups - 1):
            zz = far(s)
            arrived(recvbuf.at[zz, b], o_recv.at[zz, b])
            unpack(zz, b)
    left(gath.at[:, 0 : groups - 1, 0], z_send.at[0])
    left(gath.at[:, 0 : groups - 1], d_send.at[0])
    left(sendbuf.at[:, 0 : groups - 1], o_send.at[0])
    left(sendbuf.at[:, 0, 0], o_send.at[1])
    left(other_pairs, pair_send.at[0])
    left(other_ints, pair_send.at[1])


def fused(groups, integrals, amplitudes, occupied_energy, virtual_energy, virtual_pairs, occupied_pairs):
    nblk, nef, vec, nij = amplitudes.shape
    here, nab, _ = integrals.shape
    rows = vec * nij
    chips = lax.axis_size("dev") // 2
    amps = jnp.transpose(amplitudes, (0, 2, 3, 1)).reshape(nblk, rows, nef)
    vpairs = jnp.transpose(virtual_pairs, (0, 2, 1))
    opairs = jnp.transpose(occupied_pairs, (1, 0))
    dims = (groups, here, vec, nij, nab, nef)
    dma = pltpu.SemaphoreType.DMA
    arrays = (integrals, amps, occupied_energy, virtual_energy, vpairs, opairs)
    result = pl.pallas_call(
        functools.partial(body, dims),
        out_shape=jax.ShapeDtypeStruct((nblk, vec, 2 * nij, nab), BF16),
        in_specs=[pl.BlockSpec(memory_space=pltpu.HBM)] * 6,
        out_specs=pl.BlockSpec(memory_space=pltpu.VMEM),
        scratch_shapes=[
            pltpu.VMEM(integrals.shape, BF16),
            pltpu.VMEM(amps.shape, BF16),
            pltpu.VMEM(occupied_energy.shape, F32),
            pltpu.VMEM(virtual_energy.shape, F32),
            pltpu.VMEM(vpairs.shape, jnp.int32),
            pltpu.VMEM(opairs.shape, jnp.int32),
            pltpu.VMEM((nblk, rows // 2, LANES), BF16),
            pltpu.VMEM((here, groups, chips, 2 * rows + rows // 2, LANES), BF16),
            pltpu.VMEM(integrals.shape, BF16),
            pltpu.VMEM(vpairs.shape, jnp.int32),
            pltpu.VMEM((here, 2, nab, groups * 3 * LANES), BF16),
            pltpu.VMEM((here, 2, chips, nij, nab), F32),
            pltpu.VMEM((2 * chips * nij, LANES), F32),
            pltpu.VMEM((here, groups, 2, rows + nij, LANES), BF16),
            pltpu.VMEM((groups, here, 2, rows + nij, LANES), BF16),
            pltpu.SemaphoreType.REGULAR((3 + groups,)),
            dma((1,)),
            dma((here, groups)),
            dma((1,)),
            dma((here, groups)),
            dma((here,)),
            dma((2,)),
            dma((groups, here)),
            dma((2,)),
            dma((2,)),
            dma((2,)),
            dma((1,)),
            dma((5,)),
        ],
        compiler_params=pltpu.CompilerParams(
            collective_id=0, has_side_effects=True, vmem_limit_bytes=32 * 1024 * 1024
        ),
        name="ladder",
    )(*[pltpu.with_memory_space_constraint(array, pltpu.HBM) for array in arrays])
    return jnp.transpose(result, (0, 3, 1, 2))


def solution(mesh):
    placed = (
        P("grp", "dev", None),
        P(None, "grp", None, "dev"),
        P(),
        P(),
        P("grp", "dev", None),
        P(),
    )
    groups, devs = mesh.shape["grp"], mesh.shape["dev"]

    def local(integrals, amplitudes, *rest):
        nef, vec, nij = amplitudes.shape[1:]
        nab = integrals.shape[1]
        square = devs == 2 * 2 * 2 and devs == 2 * groups
        packs = (
            2 * LANES < nef < 3 * LANES
            and 2 * (nef % LANES) == LANES
            and LANES < nab < 2 * LANES
            and vec * (nab % LANES) == LANES
            and nij % 8 == 0
            and (vec * nij) % 32 == 0
        )
        if square and packs:
            return fused(groups, integrals, amplitudes, *rest)
        return plain(integrals, amplitudes, *rest)

    return jax.shard_map(
        local, mesh=mesh, in_specs=placed, out_specs=P(None, "dev", None, "grp"), check_vma=False
    )
```
